32 devices in a mesh: dp: 4 (over z), ctx: 2 (over core), tensor: 4 (over y, x).
Axes of the slice: x: 2, y: 2, z: 4, core: 2. Of those that a mesh axis runs over, the one named last changes fastest.
Arguments:
- tokens: bfloat16 [8, 2, 2, 256, 768], P('dp', 'ctx', None, 'tensor'), may hold values from -6 to 6
- cotangent: bfloat16 [8, 2, 2, 256, 768], P('dp', 'ctx', None, 'tensor'), may hold values from -6 to 6
- document_lengths: int32 [8, 8], P('dp'), may hold values from 1 to 512, 1024 in all within a row
- dealing: int32 [8, 7], P('dp'), may hold values from 0 to 6, each once within a row
- query_weight: bfloat16 [768, 768], P(('dp', 'ctx'), 'tensor'), may hold values from -0.21875 to 0.21875
- query_master: float32 [768, 768], P(('dp', 'ctx'), 'tensor'), may hold values from -0.21875 to 0.21875
- query_moment: float32 [768, 768], P(('dp', 'ctx'), 'tensor'), may hold values from -16 to 16
- query_variance: float32 [768, 768], P(('dp', 'ctx'), 'tensor'), may hold values from 5 to 500
- keyvalue_weight: bfloat16 [2, 768, 768], P(None, ('dp', 'ctx'), 'tensor'), may hold values from -0.21875 to 0.21875
- keyvalue_master: float32 [2, 768, 768], P(None, ('dp', 'ctx'), 'tensor'), may hold values from -0.21875 to 0.21875
- keyvalue_moment: float32 [2, 768, 768], P(None, ('dp', 'ctx'), 'tensor'), may hold values from -16 to 16
- keyvalue_variance: float32 [2, 768, 768], P(None, ('dp', 'ctx'), 'tensor'), may hold values from 5 to 500
- output_weight: bfloat16 [768, 768], P('tensor', ('dp', 'ctx')), may hold values from -1.75 to 1.75
- output_master: float32 [768, 768], P('tensor', ('dp', 'ctx')), may hold values from -1.75 to 1.75
- output_moment: float32 [768, 768], P('tensor', ('dp', 'ctx')), may hold values from -16 to 16
- output_variance: float32 [768, 768], P('tensor', ('dp', 'ctx')), may hold values from 5 to 500
- gateup_weight: bfloat16 [2, 768, 2048], P(None, ('dp', 'ctx'), 'tensor'), may hold values from -0.21875 to 0.21875
- gateup_master: float32 [2, 768, 2048], P(None, ('dp', 'ctx'), 'tensor'), may hold values from -0.21875 to 0.21875
- gateup_moment: float32 [2, 768, 2048], P(None, ('dp', 'ctx'), 'tensor'), may hold values from -16 to 16
- gateup_variance: float32 [2, 768, 2048], P(None, ('dp', 'ctx'), 'tensor'), may hold values from 5 to 500
- down_weight: bfloat16 [2048, 768], P('tensor', ('dp', 'ctx')), may hold values from -0.125 to 0.125
- down_master: float32 [2048, 768], P('tensor', ('dp', 'ctx')), may hold values from -0.125 to 0.125
- down_moment: float32 [2048, 768], P('tensor', ('dp', 'ctx')), may hold values from -16 to 16
- down_variance: float32 [2048, 768], P('tensor', ('dp', 'ctx')), may hold values from 5 to 500
- norm_gain: bfloat16 [2, 768], P(None, ('dp', 'ctx')), may hold values from 0.5 to 1.5
- gain_master: float32 [2, 768], P(None, ('dp', 'ctx', 'tensor')), may hold values from 0.5 to 1.5
- gain_moment: float32 [2, 768], P(None, ('dp', 'ctx', 'tensor')), may hold values from -16 to 16
- gain_variance: float32 [2, 768], P(None, ('dp', 'ctx', 'tensor')), may hold values from 5 to 500
Outputs:
- block_output: bfloat16 [8, 2, 2, 256, 768], P('dp', 'ctx', None, 'tensor')
- input_grad: float32 [8, 2, 2, 256, 768], P('dp', 'ctx', None, 'tensor')
- query_grad: float32 [768, 768], P(('dp', 'ctx'), 'tensor')
- master_query: float32 [768, 768], P(('dp', 'ctx'), 'tensor')
- moment_query: float32 [768, 768], P(('dp', 'ctx'), 'tensor')
- variance_query: float32 [768, 768], P(('dp', 'ctx'), 'tensor')
- keyvalue_grad: float32 [2, 768, 768], P(None, ('dp', 'ctx'), 'tensor')
- master_keyvalue: float32 [2, 768, 768], P(None, ('dp', 'ctx'), 'tensor')
- moment_keyvalue: float32 [2, 768, 768], P(None, ('dp', 'ctx'), 'tensor')
- variance_keyvalue: float32 [2, 768, 768], P(None, ('dp', 'ctx'), 'tensor')
- output_grad: float32 [768, 768], P('tensor', ('dp', 'ctx'))
- master_output: float32 [768, 768], P('tensor', ('dp', 'ctx'))
- moment_output: float32 [768, 768], P('tensor', ('dp', 'ctx'))
- variance_output: float32 [768, 768], P('tensor', ('dp', 'ctx'))
- gateup_grad: float32 [2, 768, 2048], P(None, ('dp', 'ctx'), 'tensor')
- master_gateup: float32 [2, 768, 2048], P(None, ('dp', 'ctx'), 'tensor')
- moment_gateup: float32 [2, 768, 2048], P(None, ('dp', 'ctx'), 'tensor')
- variance_gateup: float32 [2, 768, 2048], P(None, ('dp', 'ctx'), 'tensor')
- down_grad: float32 [2048, 768], P('tensor', ('dp', 'ctx'))
- master_down: float32 [2048, 768], P('tensor', ('dp', 'ctx'))
- moment_down: float32 [2048, 768], P('tensor', ('dp', 'ctx'))
- variance_down: float32 [2048, 768], P('tensor', ('dp', 'ctx'))
- gain_grad: float32 [2, 768], P(None, ('dp', 'ctx', 'tensor'))
- master_gain: float32 [2, 768], P(None, ('dp', 'ctx', 'tensor'))
- moment_gain: float32 [2, 768], P(None, ('dp', 'ctx', 'tensor'))
- variance_gain: float32 [2, 768], P(None, ('dp', 'ctx', 'tensor'))
The draws below stay inside these ranges and needn't reach their ends.
Inputs may be any that keep to these rules, and one draw needn't show every extreme that they name: `document_lengths`: in each row the entries sum to 1024; entries 0 to 6 are the documents' lengths, the last is the padding at the row's end. Each row is a permutation of 0 to 6: document dealing[r, 0] comes first in row r, then dealing[r, 1], and so on.
All inputs are finite; a program needn't handle non-finite values.
Results may differ from the reference program's by a relative error of at most 0.02.
Values may be sent and summed in bfloat16 or wider, within the bound.
No kernel may reach another device: no remote copies, remote signals or barrier semaphores. Data moves between devices by JAX's collectives and lax.ppermute only.
A program may use at most 128 MiB of HBM per device.

```python
import math
import jax
import jax.numpy as jnp
import numpy as np
from jax import lax

D = 768
FF = 2048
H = 12
KVH = 12
HD = 64
L = 1024
SEGS = 8
STEP = 10
NDOCS = 7
Q = 256
ROWS = 8


def steps_of(rng, shape, shards, low, high):
    def one(dim, shards_of):
        draws = jax.random.uniform(jax.random.fold_in(jax.random.fold_in(rng, 6), dim), (shards_of,), jnp.float32, low / len(shards), high / len(shards))
        return jnp.repeat(jnp.exp(draws), shape[dim] // shards_of).reshape((-1,) + (1,) * (len(shape) - dim - 1))

    loudness = one(*shards[0])
    for cut in shards[1:]:
        loudness = loudness * one(*cut)
    return loudness


def split_up(count, total, reach, skew):
    loads = [(1 << 20) // math.isqrt(rank ** skew) + 1 for rank in range(2, count + 1)]
    spare, given = total - reach - (count - 1), [1] * (count - 1)
    while spare > 0:
        free = [i for i in range(count - 1) if given[i] < reach]
        pool, remaining = sum([loads[i] for i in free]), spare
        for i in free:
            addition = min(reach - given[i], max(1, remaining * loads[i] // pool), spare)
            given[i] = given[i] + addition
            spare = spare - addition
    return np.array([reach] + given)


def uneven(rng, amount, total, reach, skew):
    if amount == 2:
        one = jax.random.randint(rng, (), max(1, total - reach), min(reach, total - 1) + 1)
        return jnp.stack([one, total - one])
    tallies = jnp.asarray(split_up(amount, total, reach, skew), jnp.int32)
    couples = (amount - 1) // 2
    giver, sink = tallies[1:1 + 2 * couples:2], tallies[2:2 + 2 * couples:2]
    slack = jnp.minimum(giver - 1, reach - sink)
    shifted = jax.random.randint(jax.random.fold_in(rng, 1), (couples,), 0, 1 << 20) % (slack + 1)
    tallies = tallies.at[1:1 + 2 * couples:2].set(giver - shifted).at[2:2 + 2 * couples:2].set(sink + shifted)
    return tallies[jax.random.permutation(jax.random.fold_in(rng, 2), amount)]


def centred(own_key, dims, deviation, limit, split=(), kind=jnp.bfloat16):
    level = steps_of(own_key, dims, split, -0.22, 0.18) if split else 1.0
    entries = jax.random.normal(own_key, dims, jnp.float32) * deviation * level
    return jnp.minimum(jnp.maximum(entries, -limit), limit).astype(kind)


def setup_inputs(seed: int = 0) -> dict:
    arg_keys = jax.random.split(jax.random.key(seed), 29)
    return {
        "tokens": centred(arg_keys[0], (ROWS, 2, 2, Q, D), 1.0, 6.0, ((0, 4), (1, 2), (3, 4))),
        "cotangent": centred(arg_keys[1], (ROWS, 2, 2, Q, D), 1.0, 6.0, ((0, 4), (1, 2), (3, 4))),
        "document_lengths": jax.vmap(lambda own: uneven(own, SEGS, L, L // 2, 2))(jax.random.split(arg_keys[2], ROWS)).reshape((ROWS, SEGS)).astype(jnp.int32),
        "dealing": jax.vmap(lambda own: jax.random.permutation(own, NDOCS))(jax.random.split(arg_keys[3], ROWS)).reshape((ROWS, NDOCS)).astype(jnp.int32),
        "query_weight": centred(arg_keys[4], (D, H * HD), D ** -0.5, 0.21875, ((0, 8), (1, 4))),
        "query_master": centred(arg_keys[5], (D, H * HD), D ** -0.5, 0.21875, ((0, 8), (1, 4)), jnp.float32),
        "query_moment": centred(arg_keys[6], (D, H * HD), 3.0, 16.0, ((0, 8), (1, 4)), jnp.float32),
        "query_variance": jnp.clip(jnp.exp(math.log(500.0) - 4.6051702 * jax.random.uniform(arg_keys[7], (D, H * HD), jnp.float32) ** steps_of(arg_keys[7], (D, H * HD), ((0, 8), (1, 4)), -0.2, 0.2)), 5.0, 500.0),
        "keyvalue_weight": centred(arg_keys[8], (2, D, KVH * HD), D ** -0.5, 0.21875, ((1, 8), (2, 4))),
        "keyvalue_master": centred(arg_keys[9], (2, D, KVH * HD), D ** -0.5, 0.21875, ((1, 8), (2, 4)), jnp.float32),
        "keyvalue_moment": centred(arg_keys[10], (2, D, KVH * HD), 3.0, 16.0, ((1, 8), (2, 4)), jnp.float32),
        "keyvalue_variance": jnp.clip(jnp.exp(math.log(500.0) - 4.6051702 * jax.random.uniform(arg_keys[11], (2, D, KVH * HD), jnp.float32) ** steps_of(arg_keys[11], (2, D, KVH * HD), ((1, 8), (2, 4)), -0.2, 0.2)), 5.0, 500.0),
        "output_weight": centred(arg_keys[12], (H * HD, D), (H * HD // 64) ** -0.5, 1.75, ((0, 4), (1, 8))),
        "output_master": centred(arg_keys[13], (H * HD, D), (H * HD // 64) ** -0.5, 1.75, ((0, 4), (1, 8)), jnp.float32),
        "output_moment": centred(arg_keys[14], (H * HD, D), 3.0, 16.0, ((0, 4), (1, 8)), jnp.float32),
        "output_variance": jnp.clip(jnp.exp(math.log(500.0) - 4.6051702 * jax.random.uniform(arg_keys[15], (H * HD, D), jnp.float32) ** steps_of(arg_keys[15], (H * HD, D), ((0, 4), (1, 8)), -0.2, 0.2)), 5.0, 500.0),
        "gateup_weight": centred(arg_keys[16], (2, D, FF), D ** -0.5, 0.21875, ((1, 8), (2, 4))),
        "gateup_master": centred(arg_keys[17], (2, D, FF), D ** -0.5, 0.21875, ((1, 8), (2, 4)), jnp.float32),
        "gateup_moment": centred(arg_keys[18], (2, D, FF), 3.0, 16.0, ((1, 8), (2, 4)), jnp.float32),
        "gateup_variance": jnp.clip(jnp.exp(math.log(500.0) - 4.6051702 * jax.random.uniform(arg_keys[19], (2, D, FF), jnp.float32) ** steps_of(arg_keys[19], (2, D, FF), ((1, 8), (2, 4)), -0.2, 0.2)), 5.0, 500.0),
        "down_weight": centred(arg_keys[20], (FF, D), FF ** -0.5, 0.125, ((0, 4), (1, 8))),
        "down_master": centred(arg_keys[21], (FF, D), FF ** -0.5, 0.125, ((0, 4), (1, 8)), jnp.float32),
        "down_moment": centred(arg_keys[22], (FF, D), 3.0, 16.0, ((0, 4), (1, 8)), jnp.float32),
        "down_variance": jnp.clip(jnp.exp(math.log(500.0) - 4.6051702 * jax.random.uniform(arg_keys[23], (FF, D), jnp.float32) ** steps_of(arg_keys[23], (FF, D), ((0, 4), (1, 8)), -0.2, 0.2)), 5.0, 500.0),
        "norm_gain": jnp.clip(1.0 + 0.1 * jax.random.normal(arg_keys[24], (2, D), jnp.float32), 0.5, 1.5).astype(jnp.bfloat16),
        "gain_master": jnp.clip(1.0 + 0.1 * jax.random.normal(arg_keys[25], (2, D), jnp.float32), 0.5, 1.5),
        "gain_moment": centred(arg_keys[26], (2, D), 3.0, 16.0, ((1, 32),), jnp.float32),
        "gain_variance": jnp.clip(jnp.exp(math.log(500.0) - 4.6051702 * jax.random.uniform(arg_keys[27], (2, D), jnp.float32) ** steps_of(arg_keys[27], (2, D), ((1, 32),), -0.2, 0.2)), 5.0, 500.0),
    }


@jax.custom_vjp
def low(v):
    return lax.optimization_barrier(v.astype(jnp.bfloat16)).astype(jnp.float32)

@jax.custom_vjp
def low_back(v):
    return v

def low_keep(v):
    return (low(v), None)

def low_pass(kept, grad):
    return (grad,)

def back_keep(v):
    return (v, None)

def back_low(kept, grad):
    return (low(grad),)
low.defvjp(low_keep, low_pass)
low_back.defvjp(back_keep, back_low)
EPSILON = 1e-05
BETA_ONE = 0.9
BETA_TWO = 0.95
ADAM_EPSILON = 1e-08
WEIGHT_DECAY = 0.1
LEARNING_RATE = 0.01
OUTPUT_RATE = 0.08
GAIN_RATE = 0.4
ROTARY_BASE = 10000.0
NEGATIVE = -1e+30

def product(left, right):
    return jnp.dot(left, right, precision=lax.Precision.HIGHEST)

def normed(hidden, gain):
    return hidden * lax.rsqrt(lax.optimization_barrier(jnp.mean(hidden * hidden, axis=-1, keepdims=True)) + EPSILON) * gain

def angles(position, head_width):
    half_width = head_width // 2
    inverse = ROTARY_BASE ** (-(jnp.arange(half_width, dtype=jnp.float32) * 2.0 / head_width))
    phase = position.astype(jnp.float32)[..., None] * inverse
    return (jnp.cos(phase), jnp.sin(phase))

def rotate(values, cosine, sine):
    half_width = values.shape[-1] // 2
    former = values[..., :half_width]
    latter = values[..., half_width:]
    cosine = cosine[..., None, :]
    sine = sine[..., None, :]
    return jnp.concatenate([former * cosine - latter * sine, latter * cosine + former * sine], axis=-1)

def document_ends(lengths, dealing):
    documents = dealing.shape[-1]
    picked = (dealing[..., :, None] == jnp.arange(documents, dtype=jnp.int32)).astype(jnp.int32)
    placed = lax.optimization_barrier(jnp.sum(picked * lengths[..., None, :documents], axis=-1))
    return jnp.cumsum(placed, axis=-1).astype(jnp.int32)

def locate(position, ends):
    after = position[..., None] >= ends
    segment = lax.optimization_barrier(jnp.sum(after.astype(jnp.int32), axis=-1))
    begin = lax.optimization_barrier(jnp.max(jnp.where(after, ends, 0), axis=-1))
    return (segment, position - begin)

def natural(paired_rows):
    return jnp.concatenate([paired_rows[:, 0, 0], paired_rows[:, 1, 0], paired_rows[:, 1, 1], paired_rows[:, 0, 1]], axis=1)

def paired_quarters(natural_rows):
    quarter_size = natural_rows.shape[1] // 4
    pieces = [natural_rows[:, index * quarter_size:(index + 1) * quarter_size] for index in range(4)]
    former = jnp.stack([pieces[0], pieces[3]], axis=1)
    latter = jnp.stack([pieces[1], pieces[2]], axis=1)
    return jnp.stack([former, latter], axis=1)

def row_forward(hidden, query_full, keyvalue_full, output_full, gateup_full, down_full, gains, segment, position):
    first_norm = low(normed(hidden, gains[0]))
    query_raw = low_back(product(first_norm, query_full))
    key_raw = low_back(product(first_norm, keyvalue_full[0]))
    values_all = low(low_back(product(first_norm, keyvalue_full[1]))).reshape(L, KVH, HD)
    cosine, sine = angles(position, HD)
    queries = low(rotate(query_raw.reshape(L, H, HD), cosine, sine)).reshape(L, KVH, H // KVH, HD)
    keys_all = low(rotate(key_raw.reshape(L, KVH, HD), cosine, sine))
    scores = low_back(jnp.einsum('qkgd,tkd->kgqt', queries, keys_all, precision=lax.Precision.HIGHEST))
    indices = jnp.arange(L, dtype=jnp.int32)
    allowed = (segment[:, None] == segment[None, :]) & (indices[:, None] >= indices[None, :])
    probability = jax.nn.softmax(jnp.where(allowed, scores * HD ** (-0.5), NEGATIVE), axis=-1)
    mixture = jnp.einsum('kgqt,tkd->qkgd', low(probability), values_all, precision=lax.Precision.HIGHEST)
    mixture = low(low_back(mixture.reshape(L, H * HD)))
    middle = hidden + low_back(product(mixture, output_full))
    second_norm = low(normed(middle, gains[1]))
    gating = low_back(product(second_norm, gateup_full[0]))
    upward = low_back(product(second_norm, gateup_full[1]))
    active = low(jax.nn.silu(gating) * upward)
    return middle + low_back(product(active, down_full))

def adam_step(gradient, master, moment, variance, decay, rate):
    moment_new = BETA_ONE * moment + (1.0 - BETA_ONE) * gradient
    variance_new = BETA_TWO * variance + (1.0 - BETA_TWO) * gradient * gradient
    first_fix = 1.0 - BETA_ONE ** STEP
    second_fix = 1.0 - BETA_TWO ** STEP
    stepped = moment_new / first_fix / (jnp.sqrt(variance_new / second_fix) + ADAM_EPSILON) + decay * master
    return (master - rate * stepped, moment_new, variance_new)

def reference(tokens, cotangent, document_lengths, dealing, query_weight, query_master, query_moment, query_variance, keyvalue_weight, keyvalue_master, keyvalue_moment, keyvalue_variance, output_weight, output_master, output_moment, output_variance, gateup_weight, gateup_master, gateup_moment, gateup_variance, down_weight, down_master, down_moment, down_variance, norm_gain, gain_master, gain_moment, gain_variance):
    inputs_rows = natural(tokens.astype(jnp.float32))
    grads_rows = natural(cotangent.astype(jnp.float32))
    weights = (query_weight.astype(jnp.float32), keyvalue_weight.astype(jnp.float32), output_weight.astype(jnp.float32), gateup_weight.astype(jnp.float32), down_weight.astype(jnp.float32), norm_gain.astype(jnp.float32))
    ends = document_ends(document_lengths, dealing)

    def one_row(totals, items):
        hidden, grad_rows, row_ends = items
        indices = jnp.arange(L, dtype=jnp.int32)
        segment, position = locate(indices, row_ends)
        keep_mask = (indices < row_ends[-1]).astype(jnp.float32)

        def forward(hidden_in, *params):
            return row_forward(hidden_in, *params, segment, position)
        result, pull = jax.vjp(forward, hidden, *weights)
        gradients = pull(grad_rows * keep_mask[:, None])
        totals = tuple((accrued + fresh_grad for accrued, fresh_grad in zip(totals, gradients[1:])))
        return (totals, (result.astype(jnp.bfloat16), gradients[0]))
    zeros = tuple((jnp.zeros(weight_item.shape, jnp.float32) for weight_item in weights))
    totals, (outputs_rows, input_rows) = lax.scan(one_row, zeros, (inputs_rows, grads_rows, ends))
    query_grad, keyvalue_grad, output_grad, gateup_grad, down_grad, gain_grad = totals
    query_new = adam_step(query_grad, query_master, query_moment, query_variance, WEIGHT_DECAY, LEARNING_RATE)
    keyvalue_new = adam_step(keyvalue_grad, keyvalue_master, keyvalue_moment, keyvalue_variance, WEIGHT_DECAY, LEARNING_RATE)
    output_new = adam_step(output_grad, output_master, output_moment, output_variance, WEIGHT_DECAY, OUTPUT_RATE)
    gateup_new = adam_step(gateup_grad, gateup_master, gateup_moment, gateup_variance, WEIGHT_DECAY, LEARNING_RATE)
    down_new = adam_step(down_grad, down_master, down_moment, down_variance, WEIGHT_DECAY, LEARNING_RATE)
    gain_new = adam_step(gain_grad, gain_master, gain_moment, gain_variance, 0.0, GAIN_RATE)
    return (paired_quarters(outputs_rows), paired_quarters(input_rows), query_grad, query_new[0], query_new[1], query_new[2], keyvalue_grad, keyvalue_new[0], keyvalue_new[1], keyvalue_new[2], output_grad, output_new[0], output_new[1], output_new[2], gateup_grad, gateup_new[0], gateup_new[1], gateup_new[2], down_grad, down_new[0], down_new[1], down_new[2], gain_grad, gain_new[0], gain_new[1], gain_new[2])
```

```python
import functools

import jax
import jax.numpy as jnp
from jax import lax
from jax.experimental import pallas as pl
from jax.experimental.pallas import tpu as pltpu
from jax.sharding import PartitionSpec as P

H = 12
HD = 64
STEP = 10
PARTS = 4
HEADS = H // PARTS
TILE = 2 * HD
QKV = 5 * TILE

EPSILON = 1e-05
BETA_ONE = 0.9
BETA_TWO = 0.95
ADAM_EPSILON = 1e-08
WEIGHT_DECAY = 0.1
LEARNING_RATE = 0.01
OUTPUT_RATE = 0.08
GAIN_RATE = 0.4
ROTARY_BASE = 10000.0
NEGATIVE = -1e30

F32 = jnp.float32
BF16 = jnp.bfloat16
SMEM = pl.BlockSpec(memory_space=pltpu.SMEM)
VMEM = pl.BlockSpec(memory_space=pltpu.VMEM)


def call(name, body, outs, scalars, arrays, scratch=(), grown=None):
    extra = () if grown is None else (grown,)
    out_shape = [jax.ShapeDtypeStruct(shape, dtype) for shape, dtype in outs]
    out_shape += [jax.ShapeDtypeStruct(value.shape, value.dtype) for value in extra]
    anywhere = [pl.BlockSpec(memory_space=pl.ANY) for _ in extra]
    scratch_shapes = [pltpu.VMEM(shape, dtype) for shape, dtype in scratch]
    if extra:
        scratch_shapes.append(pltpu.SemaphoreType.DMA(()))
    position = len(scalars) + len(arrays)
    return pl.pallas_call(
        body,
        out_shape=out_shape,
        in_specs=[SMEM] * len(scalars) + [VMEM] * len(arrays) + anywhere,
        out_specs=[VMEM] * len(outs) + anywhere,
        scratch_shapes=scratch_shapes,
        input_output_aliases={position: len(outs)} if extra else {},
        compiler_params=pltpu.CompilerParams(vmem_limit_bytes=60 << 20),
        name=name,
    )(*scalars, *arrays, *extra)


def dot(left, right):
    return lax.dot_general(left, right, (((1,), (0,)), ((), ())), preferred_element_type=F32)


def dot_nt(left, right):
    return lax.dot_general(left, right, (((1,), (1,)), ((), ())), preferred_element_type=F32)


def dot_tn(left, right):
    return lax.dot_general(left, right, (((0,), (0,)), ((), ())), preferred_element_type=F32)


def rows_at(start, size, unit):
    return pl.ds(pl.multiple_of(start, unit), size)


def lanes_of(shape):
    return lax.broadcasted_iota(jnp.int32, shape, len(shape) - 1)


def swapped(tile):
    first = (lanes_of(tile.shape) % HD) < HD // 2
    return jnp.where(first, pltpu.roll(tile, TILE - HD // 2, 1), pltpu.roll(tile, HD // 2, 1))


def root_mean(values):
    return lax.rsqrt(jnp.mean(values * values, axis=-1, keepdims=True) + EPSILON)


def stack_body(meta, *refs):
    pieces, out = refs[:-1], refs[-1]
    count = len(pieces)
    for shift, piece in enumerate(pieces):
        out[lax.rem(meta[2] + count - shift, count)] = piece[...]


def assemble(meta, own, other, target, low, high):
    context = meta[1]
    count, rows, _ = own.shape
    for index in range(count):
        target[rows_at((2 * index + context) * rows, rows, 16), :] = own[index, :, low:high]
        target[rows_at((2 * index + 1 - context) * rows, rows, 16), :] = other[index, :, low:high]


def assemble_first_body(meta, own, other, weight, gains):
    assemble(meta, own, other, weight, 0, QKV)
    tile = weight[:, TILE : 2 * TILE].astype(F32)
    gains[...] = tile.T[HD : HD + 8, :]
    weight[:, TILE : 2 * TILE] = jnp.where(lanes_of(tile.shape) < HD, tile, 0.0).astype(BF16)


def project_body(
    meta, x0, x1, x2, x3, x4, gains, weight, cosine, sine, hidden, normed, query, keyval
):
    part = meta[0]
    blocks = x0.shape[0] // 64
    gain = gains[0:1, :]
    pieces = ((x0, 0, 0), (x1, 1, 0), (x2, 2, 0), (x3, 3, 0), (x4, 3, blocks // 2))
    for piece, offset, start in pieces:
        place = jnp.bitwise_xor(part, offset)

        def spread(block, carry, piece=piece, place=place, start=start):
            source = piece[rows_at(block * 64, 64, 64), :]
            values = source.astype(F32)
            target = rows_at((start + block) * 256 + place * 64, 64, 64)
            hidden[target, :] = source
            normed[target, :] = (values * root_mean(values) * gain).astype(BF16)
            return carry

        lax.fori_loop(0, piece.shape[0] // 64, spread, 0)

    def rotate(block, carry):
        rows = rows_at(block * 256, 256, 256)
        raw = dot(normed[rows, :], weight[...])
        cos, sin = cosine[rows, :], sine[rows, :]
        lower = lanes_of(cos.shape) < HD
        for index in range(5):
            tile = raw[:, index * TILE : (index + 1) * TILE]
            turned = tile * cos + swapped(tile) * sin
            lanes = slice((index - 2) * TILE, (index - 1) * TILE)
            if index < 2:
                query[rows, index * TILE : (index + 1) * TILE] = (turned * HD**-0.5).astype(BF16)
            else:
                keyval[rows, lanes] = jnp.where(lower, turned, tile).astype(BF16)
        return carry

    lax.fori_loop(0, blocks, rotate, 0)


def gather_keys(context, row, own, other, absolute):
    for side in range(2):
        rows = rows_at(row * 512 + side * 256, 256, 256)
        mine = context if side == 0 else 3 - context
        theirs = 1 - context if side == 0 else 2 + context
        absolute[mine] = own[rows, :]
        absolute[theirs] = other[rows, :]


def mask_bias(ends, row, query_quarter, key_quarter, documents):
    query_point = query_quarter * 256 + lax.broadcasted_iota(jnp.int32, (1, 256), 1)
    begin = jnp.zeros((1, 256), jnp.int32)
    for index in range(documents):
        end = ends[row, index]
        begin = jnp.where(query_point >= end, jnp.maximum(begin, end), begin)
    key_point = key_quarter * 256 + lax.broadcasted_iota(jnp.int32, (256, 256), 0)
    return jnp.where((key_point <= query_point) & (key_point >= begin), 0.0, NEGATIVE)


def query_pads(tiles):
    first, second = tiles[:, :TILE].astype(F32), tiles[:, TILE:].astype(F32)
    lower = lanes_of(first.shape) < HD
    return [
        jnp.where(lower, first, 0.0).astype(BF16),
        jnp.where(lower, pltpu.roll(first, HD, 1), 0.0).astype(BF16),
        jnp.where(lower, second, 0.0).astype(BF16),
    ]


def attend_body(meta, ends, query, own, other, mixed, logs, keys, keys_turned, bias, scores):
    context = meta[1]
    documents = ends.shape[1]

    def one(row, carry):
        gather_keys(context, row, own, other, keys)
        for quarter in range(4):
            for head in range(HEADS):
                lanes = slice(head * TILE, (head + 1) * TILE)
                keys_turned[quarter, lanes, :] = keys[quarter, :, lanes].astype(F32).T.astype(BF16)
        outs = []
        for side in range(2):
            quarter = context if side == 0 else 3 - context
            count = 2 + side
            base = 0 if side == 0 else 1 - context
            rows = rows_at(row * 512 + side * 256, 256, 256)
            for step in range(count):
                bias[step] = mask_bias(ends, meta[3] + row, quarter, base + step, documents)
            pads = query_pads(query[rows, :])
            turned = []
            for head in range(HEADS):
                lanes = slice(head * TILE, (head + 1) * TILE)
                highest = jnp.full((1, 256), NEGATIVE, F32)
                for step in range(count):
                    value = dot_nt(keys[base + step, :, lanes], pads[head]) + bias[step]
                    scores[step] = value
                    highest = jnp.maximum(highest, jnp.max(value, axis=0, keepdims=True))
                total = jnp.zeros((1, 256), F32)
                for step in range(count):
                    value = jnp.exp(scores[step] - highest)
                    scores[step] = value
                    total = total + jnp.sum(value, axis=0, keepdims=True)
                inverse = 1.0 / total
                result = jnp.zeros((TILE, 256), F32)
                for step in range(count):
                    weights = (scores[step] * inverse).astype(BF16)
                    result = result + dot(keys_turned[base + step, lanes, :], weights)
                turned.append(result[HD:, :])
                logs[2 * row + side, head : head + 1, :] = highest + jnp.log(total)
            pair = jnp.concatenate(turned[:2], axis=0)
            mixed[rows_at(row * 768 + side * 256, 256, 256), :] = pair.T.astype(BF16)
            outs.append(turned[2])
        packed = jnp.concatenate(outs, axis=0)
        mixed[rows_at(row * 768 + 512, 256, 256), :] = packed.T.astype(BF16)
        return carry

    lax.fori_loop(0, query.shape[0] // 512, one, 0)


def silu_parts(gating):
    gate = 1.0 / (1.0 + jnp.exp(-gating))
    return gate, gating * gate


def joined_heads(row, side, heads, target, lower):
    start = row * 768 + side * 256
    for index in range(PARTS):
        target[:, index * TILE : (index + 1) * TILE] = heads[index][start : start + 256, :]
    for index in range(2):
        tail = slice(row * 768 + 512, row * 768 + 768)
        left = heads[2 * index][tail, :].astype(F32)
        right = heads[2 * index + 1][tail, :].astype(F32)
        if side == 0:
            tile = jnp.where(lower, left, pltpu.roll(right, HD, 1))
        else:
            tile = jnp.where(lower, pltpu.roll(left, HD, 1), right)
        target[:, (PARTS + index) * TILE : (PARTS + index + 1) * TILE] = tile.astype(BF16)


def feed_body(
    meta, ends, hidden, h0, h1, h2, h3, c0, c1, c2, c3, gains, output, gateup, down,
    o0, o1, o2, o3, second, active, grads, spread, middle_own, heads_own,
    joined, block_grad, block_middle,
):
    part, context = meta[0], meta[1]
    width = down.shape[1]
    gain = gains[1:2, :]
    lower = lanes_of((256, TILE)) < HD
    for row in range(hidden.shape[0] // 512):
        for side in range(2):
            block = 2 * row + side
            rows = slice(block * 256, block * 256 + 256)
            joined_heads(row, side, (h0, h1, h2, h3), joined, lower)
            for offset, piece in enumerate((c0, c1, c2, c3)):
                place = jnp.bitwise_xor(part, offset)
                target = rows_at(block * 256 + place * 64, 64, 64)
                spread[target, :] = piece[block * 64 : block * 64 + 64, :]
            quarter = context if side == 0 else 3 - context
            point = quarter * 256 + lax.broadcasted_iota(jnp.int32, (256, 1), 0)
            keep = point < ends[meta[3] + row, ends.shape[1] - 1]
            out_grad = jnp.where(keep, spread[rows, :].astype(F32), 0.0).astype(BF16)
            spread[rows, :] = out_grad
            middle = hidden[rows, :].astype(F32) + dot_nt(joined[...], output[...])
            block_middle[...] = middle
            normed = (middle * root_mean(middle) * gain).astype(BF16)
            second[rows, :] = normed
            own = slice(block * 64, block * 64 + 64)
            mine = rows_at(part * 64, 64, 64)
            middle_own[own, :] = block_middle[mine, :]
            heads_own[own, :] = joined[mine, :]
            gate_up = dot(normed, gateup[...])
            gating, upward = gate_up[:, :width], gate_up[:, width:]
            grad_active = dot(out_grad, down[...])
            gate, passed = silu_parts(gating)
            active[rows, :] = (passed * upward).astype(BF16)
            grads[rows, :width] = (
                grad_active * upward * gate * (1.0 + gating * (1.0 - gate))
            ).astype(BF16)
            grads[rows, width:] = (grad_active * passed).astype(BF16)
            block_grad[...] = dot_nt(grads[rows, :], gateup[...]).astype(BF16)
            for offset, piece in enumerate((o0, o1, o2, o3)):
                place = jnp.bitwise_xor(part, offset)
                piece[own, :] = block_grad[rows_at(place * 64, 64, 64), :]


def fed_body(meta, active, down, out, block_out):
    for block in range(active.shape[0] // 256):
        rows = slice(block * 256, block * 256 + 256)
        block_out[...] = dot_nt(active[rows, :], down[...]).astype(BF16)
        for place in range(PARTS):
            out[place, block * 64 : block * 64 + 64, :] = block_out[place * 64 : place * 64 + 64, :]


def split_rows(context, source, keep, send, lanes):
    count, rows, _ = keep.shape
    for index in range(count):
        keep[index, :, lanes] = source[rows_at((2 * index + context) * rows, rows, 32), :]
        send[index, :, lanes] = source[
            rows_at((2 * index + 1 - context) * rows, rows, 32), :
        ].astype(BF16)


def feed_weights_body(meta, *refs):
    blocks = (len(refs) - 3) // 4
    second, grads, active, spread = (refs[i * blocks : (i + 1) * blocks] for i in range(4))
    out, left, right = refs[4 * blocks :]
    turned = 0
    for normed, grad in zip(second, spread):
        for block in range(normed.shape[0] // 256):
            rows = slice(block * 256, block * 256 + 256)
            lanes = slice(turned * 256, turned * 256 + 256)
            left[:, lanes] = normed[rows, :].T
            right[:, lanes] = grad[rows, :].T
            turned += 1
    width = active[0].shape[1]
    for start in range(0, 3 * width, 256):
        total = None
        offset = 0
        for index in range(blocks):
            size = second[index].shape[0]
            span = slice(offset, offset + size)
            if start < 2 * width:
                value = dot(left[:, span], grads[index][:, start : start + 256])
            else:
                first = start - 2 * width
                value = dot(right[:, span], active[index][:, first : first + 256])
            total = value if total is None else total + value
            offset += size
        out[:, start : start + 256] = total.astype(BF16)


def middle_body(
    meta, ends, g0, g1, g2, g3, middle_ref, out_grad_ref, gains, output,
    s0, s1, s2, s3, grad_ref, low_ref, gain_ref,
):
    part, context = meta[0], meta[1]
    total = g0[...].astype(F32) + g1[...].astype(F32) + g2[...].astype(F32) + g3[...].astype(F32)
    middle = middle_ref[...]
    scale = root_mean(middle)
    gain = gains[1:2, :]
    keeps = []
    for block in range(middle.shape[0] // 64):
        row, side = block // 2, block % 2
        quarter = context if side == 0 else 3 - context
        point = quarter * 256 + part * 64 + lax.broadcasted_iota(jnp.int32, (64, 1), 0)
        keeps.append(point < ends[meta[3] + row, ends.shape[1] - 1])
    keep = jnp.concatenate([value.astype(F32) for value in keeps], axis=0)
    out_grad = out_grad_ref[...].astype(F32) * keep
    scaled = gain * total
    inner = jnp.mean(scaled * middle, axis=-1, keepdims=True)
    grad = out_grad + scale * scaled - middle * (scale * scale * scale * inner)
    grad_ref[...] = grad
    low = grad.astype(BF16)
    low_ref[...] = low
    gain_ref[...] = jnp.broadcast_to(
        jnp.sum(total * middle * scale, axis=0, keepdims=True), gain_ref.shape
    )
    heads = dot(low, output[...])
    lower = lanes_of((64, TILE)) < HD
    for offset, piece in enumerate((s0, s1, s2, s3)):
        tail = PARTS + offset // 2
        for row in range(middle.shape[0] // 128):
            rows = slice(row * 128, row * 128 + 128)
            piece[row * 192 : row * 192 + 128, :] = heads[
                rows, offset * TILE : (offset + 1) * TILE
            ].astype(BF16)
            former = heads[row * 128 : row * 128 + 64, tail * TILE : (tail + 1) * TILE]
            latter = heads[row * 128 + 64 : row * 128 + 128, tail * TILE : (tail + 1) * TILE]
            if offset % 2 == 0:
                packed = jnp.where(lower, former, pltpu.roll(latter, HD, 1))
            else:
                packed = jnp.where(lower, pltpu.roll(former, HD, 1), latter)
            piece[row * 192 + 128 : row * 192 + 192, :] = packed.astype(BF16)


def output_weights_body(meta, low, heads, grown_in, grown, tile, arrived):
    turned = low[...].T
    width = tile.shape[1]
    for start in range(0, width, 256):
        tile[:, start : start + 256] = dot(turned, heads[:, start : start + 256]).astype(BF16)
    copy = pltpu.make_async_copy(tile, grown.at[:, pl.ds(grown.shape[1] - width, width)], arrived)
    copy.start()
    copy.wait()


def attend_back_body(
    meta, ends, query, own, other, g0, g1, g2, g3, logs, cosine, sine,
    grad_query, grad_own, grad_other, keys, keys_turned, bias, grad_heads, probs, grad_probs, sums,
):
    part, context = meta[0], meta[1]
    documents = ends.shape[1]

    def one(row, carry):
        gather_keys(context, row, own, other, keys)
        sums[...] = jnp.zeros_like(sums)
        for quarter in range(4):
            for head in range(HEADS):
                lanes = slice(head * TILE, (head + 1) * TILE)
                keys_turned[quarter, lanes, :] = keys[quarter, :, lanes].astype(F32).T.astype(BF16)
        for offset, piece in enumerate((g0, g1, g2, g3)):
            place = jnp.bitwise_xor(part, offset)
            for side in range(2):
                start = row * 192 + side * 64
                grad_heads[side, rows_at(place * 64, 64, 64), :TILE] = piece[rows_at(start, 64, 64), :]
            grad_heads[0, rows_at(place * 64, 64, 64), TILE:] = piece[
                rows_at(row * 192 + 128, 64, 64), :
            ]
        for side in range(2):
            quarter = context if side == 0 else 3 - context
            count = 2 + side
            base = 0 if side == 0 else 1 - context
            rows = rows_at(row * 512 + side * 256, 256, 256)
            for step in range(count):
                bias[step] = mask_bias(ends, meta[3] + row, quarter, base + step, documents)
            pads = query_pads(query[rows, :])
            first = grad_heads[side, :, :TILE].astype(F32)
            second = grad_heads[0, :, TILE:].astype(F32)
            upper = lanes_of(first.shape) >= HD
            tail = pltpu.roll(second, HD, 1) if side == 0 else second
            grads = [
                jnp.where(upper, pltpu.roll(first, HD, 1), 0.0).astype(BF16),
                jnp.where(upper, first, 0.0).astype(BF16),
                jnp.where(upper, tail, 0.0).astype(BF16),
            ]
            turned = []
            for head in range(HEADS):
                lanes = slice(head * TILE, (head + 1) * TILE)
                log = logs[2 * row + side, head : head + 1, :]
                inner = jnp.zeros((1, 256), F32)
                for step in range(count):
                    block = keys[base + step, :, lanes]
                    chance = jnp.exp(dot_nt(block, pads[head]) + bias[step] - log)
                    slope = dot_nt(block, grads[head])
                    probs[step] = chance
                    grad_probs[step] = slope
                    inner = inner + jnp.sum(chance * slope, axis=0, keepdims=True)
                sides = jnp.concatenate([pads[head], grads[head]], axis=0)
                result = jnp.zeros((TILE, 256), F32)
                for step in range(count):
                    chance = probs[step]
                    slope = (chance * (grad_probs[step] - inner)).astype(BF16)
                    both = jnp.concatenate([slope, chance.astype(BF16)], axis=1)
                    sums[base + step, :, lanes] += dot(both, sides)
                    result = result + dot(keys_turned[base + step, lanes, :], slope)
                turned.append(result[:HD, :])
            cos, sin = cosine[rows, :], sine[rows, :]
            turned.append(jnp.zeros((HD, 256), F32))
            for index in range(2):
                tile = jnp.concatenate(turned[2 * index : 2 * index + 2], axis=0).T * HD**-0.5
                grad_query[rows, index * TILE : (index + 1) * TILE] = (
                    tile * cos - swapped(tile) * sin
                ).astype(BF16)
        for side in range(2):
            rows = rows_at(row * 512 + side * 256, 256, 256)
            mine = context if side == 0 else 3 - context
            theirs = 1 - context if side == 0 else 2 + context
            grad_own[rows, :] = sums[mine]
            grad_other[rows, :] = sums[theirs].astype(BF16)
        return carry

    lax.fori_loop(0, query.shape[0] // 512, one, 0)


def first_body(meta, grad_query, grad_own, arrived, cosine, sine, grads):
    def one(block, carry):
        rows = rows_at(block * 256, 256, 256)
        cos, sin = cosine[rows, :], sine[rows, :]
        lower = lanes_of(cos.shape) < HD
        grads[rows, : 2 * TILE] = grad_query[rows, :]
        for index in range(HEADS):
            lanes = slice(index * TILE, (index + 1) * TILE)
            tile = grad_own[rows, lanes] + arrived[rows, lanes].astype(F32)
            turned = tile * cos - swapped(tile) * sin
            grads[rows, (2 + index) * TILE : (3 + index) * TILE] = jnp.where(
                lower, turned, tile
            ).astype(BF16)
        return carry

    lax.fori_loop(0, grad_query.shape[0] // 256, one, 0)


def spread_grad_body(meta, grads, weight, out, block_grad):
    def one(block, carry):
        rows = rows_at(block * 256, 256, 256)
        block_grad[...] = dot_nt(grads[rows, :], weight[...]).astype(BF16)
        for place in range(PARTS):
            target = rows_at(block * 64, 64, 64)
            out[place, target, :] = block_grad[place * 64 : place * 64 + 64, :]
        return carry

    lax.fori_loop(0, grads.shape[0] // 256, one, 0)


def first_weights_body(meta, normed, grads, weight, gains, gain_two, *refs):
    outs, total, turned = refs[:-2], refs[-2], refs[-1]
    turned[...] = normed[...].T
    width = total.shape[1]
    for start in range(0, width, TILE):
        lanes = slice(start, start + TILE)
        total[:, lanes] = dot(turned[...], grads[:, lanes])
    product = total[...] * weight[...].astype(F32)
    column = jnp.sum(product, axis=1, keepdims=True)
    lane = lanes_of((normed.shape[1], TILE))
    row = lax.broadcasted_iota(jnp.int32, (TILE, normed.shape[1]), 0)
    two = jnp.where(row == HD + 1, gain_two[0:1, :], 0.0)
    one = jnp.where(row == HD, 1.0 / gains[0:1, :], 0.0)
    total[:, TILE : 2 * TILE] += two.T + one.T * column
    if len(outs) == 2:
        split_rows(meta[1], total, *outs, slice(0, width))
    else:
        outs[0][...] = total[...].astype(BF16)


def input_body(meta, landed, tokens, grad_middle, gains, out):
    total = landed[0].astype(F32)
    for index in range(1, PARTS):
        total = total + landed[index].astype(F32)
    values = tokens[...].astype(F32)
    scale = root_mean(values)
    scaled = gains[0:1, :] * total
    inner = jnp.mean(scaled * values, axis=-1, keepdims=True)
    out[...] = grad_middle[...] + scale * scaled - values * (scale * scale * scale * inner)


def context_sum_body(meta, keep, arrived, *outs):
    count = len(outs)
    for shift, out in enumerate(outs):
        index = lax.rem(meta[2] + shift, count)
        out[...] = (keep[index] + arrived[index].astype(F32)).astype(out.dtype)


def document_ends(lengths, dealing):
    documents = dealing.shape[-1]
    picked = (dealing[..., :, None] == jnp.arange(documents, dtype=jnp.int32)).astype(jnp.int32)
    placed = jnp.sum(picked * lengths[..., None, :documents], axis=-1)
    return jnp.cumsum(placed, axis=-1)


def rotary_tables(ends, context):
    inverse = ROTARY_BASE ** (-(jnp.arange(HD // 2, dtype=F32) * 2.0 / HD))
    inverse = jnp.tile(inverse, 4)
    inner = jnp.arange(256, dtype=jnp.int32)
    points = jnp.stack([context * 256 + inner, (3 - context) * 256 + inner]).reshape(1, 512)
    after = points[..., None] >= ends[:, None, :]
    position = points - jnp.max(jnp.where(after, ends[:, None, :], 0), axis=-1)
    phase = position.astype(F32).reshape(-1, 1) * inverse
    sign = jnp.where((jnp.arange(TILE) % HD) < HD // 2, -1.0, 1.0).astype(F32)
    return jnp.cos(phase), jnp.sin(phase) * sign


def adam_step(gradient, master, moment, variance, decay, rate):
    moment_new = BETA_ONE * moment + (1.0 - BETA_ONE) * gradient
    variance_new = BETA_TWO * variance + (1.0 - BETA_TWO) * gradient * gradient
    first_fix = 1.0 - BETA_ONE**STEP
    second_fix = 1.0 - BETA_TWO**STEP
    stepped = (
        moment_new / first_fix / (jnp.sqrt(variance_new / second_fix) + ADAM_EPSILON)
        + decay * master
    )
    return (gradient, master - rate * stepped, moment_new, variance_new)


def swap_ctx(value):
    return lax.ppermute(value, "ctx", [(0, 1), (1, 0)])


def across(value, offset):
    return lax.ppermute(value, "tensor", [(i, i ^ offset) for i in range(PARTS)])


def shift_dp(value, shift):
    size = lax.axis_size("dp")
    return lax.ppermute(value, "dp", [(i, (i + shift) % size) for i in range(size)])


def spread_all(value):
    return [value] + [across(value, offset) for offset in range(1, PARTS)]


def spread_in_turn(value):
    half = value.shape[0] // 2
    first, second = across(value, 1), across(value, 2)
    return [value, first, second, across(second[:half], 1), across(first[half:], 2)]


def exchange(pieces):
    return [pieces[0]] + [across(pieces[offset], offset) for offset in range(1, PARTS)]


def after(value, *others):
    return lax.optimization_barrier((value, others))[0]


class Chain:
    def __init__(self, meta):
        self.meta = meta

    def call(self, name, body, outs, scalars, arrays, scratch=(), grown=None):
        results = call(name, body, outs, (self.meta, *scalars), arrays, scratch, grown)
        self.meta = after(self.meta, results[-1])
        return results


def gather_blocks(block):
    count = lax.axis_size("dp")
    return [block] + [shift_dp(block, shift) for shift in range(1, count)]


def stack_blocks(chain, pieces):
    shape = (len(pieces), *pieces[0].shape)
    return chain.call("stack", stack_body, [(shape, BF16)], (), pieces)[0]


def context_sums(chain, keep, arrived):
    count = lax.axis_size("dp")
    _, rows, width = keep.shape
    outs = [((rows, width), F32)] + [((rows, width), BF16)] * (count - 1)
    return chain.call("context_sum", context_sum_body, outs, (), (keep, arrived))


def landed_blocks(sums):
    total = sums[0]
    for shift in range(1, len(sums)):
        total = total + shift_dp(sums[shift], shift).astype(F32)
    return total


def per_device(
    tokens,
    cotangent,
    document_lengths,
    dealing,
    query_weight,
    query_master,
    query_moment,
    query_variance,
    keyvalue_weight,
    keyvalue_master,
    keyvalue_moment,
    keyvalue_variance,
    output_weight,
    output_master,
    output_moment,
    output_variance,
    gateup_weight,
    gateup_master,
    gateup_moment,
    gateup_variance,
    down_weight,
    down_master,
    down_moment,
    down_variance,
    norm_gain,
    gain_master,
    gain_moment,
    gain_variance,
):
    features = tokens.shape[-1]
    row_count = tokens.shape[0]
    block_rows = query_weight.shape[0]
    hidden_width = down_weight.shape[0]
    block_count = lax.axis_size("dp")
    part = lax.axis_index("tensor").astype(jnp.int32)
    context = lax.axis_index("ctx").astype(jnp.int32)
    own_dp = lax.axis_index("dp").astype(jnp.int32)
    meta = jnp.stack([part, context, own_dp, jnp.int32(0)])
    ends = document_ends(document_lengths, dealing)

    chain = Chain(meta)
    own_rows = row_count * 128
    count = row_count * 512
    own_tokens = tokens.reshape(own_rows, features)
    own_grad = cotangent.reshape(own_rows, features)
    token_pieces = spread_in_turn(own_tokens)

    keys = [keyvalue_weight[i, :, h * HD : (h + 1) * HD] for h in range(HEADS) for i in range(2)]
    filler = jnp.zeros((block_rows, HD - 2), BF16)
    first_block = jnp.concatenate([query_weight, norm_gain.T, filler] + keys, axis=1)
    by_hand = block_rows % 32 == 0 and block_count <= 8
    first_pieces = gather_blocks(first_block) if by_hand else []
    output_pieces = spread_all(after(output_weight.T, token_pieces[1:3], first_pieces))
    second_block = jnp.concatenate(
        [piece[:, :TILE] for piece in output_pieces]
        + [piece[:, TILE:] for piece in output_pieces]
        + [gateup_weight[0], gateup_weight[1], down_weight.T],
        axis=1,
    )
    cosine, sine = rotary_tables(ends, context)
    second_full = lax.all_gather(second_block, ("dp", "ctx"), axis=0, tiled=True)
    if by_hand:
        first_own = stack_blocks(chain, first_pieces)
        weight, gains = chain.call(
            "assemble_first",
            assemble_first_body,
            [((features, QKV), BF16), ((8, features), F32)],
            (),
            (first_own, swap_ctx(first_own)),
        )
    else:
        first_full = lax.all_gather(first_block, ("dp", "ctx"), axis=0, tiled=True)
        gains = jnp.pad(first_full[:, 3 * HD : 3 * HD + 2].T.astype(F32), ((0, 6), (0, 0)))
        lane = jnp.arange(QKV)
        weight = jnp.where((lane >= 3 * HD) & (lane < 4 * HD), 0, first_full).astype(BF16)
    hidden, normed, query, keyval = chain.call(
        "project",
        project_body,
        [((count, features), BF16)] * 2 + [((count, 2 * TILE), BF16), ((count, 3 * TILE), BF16)],
        (),
        (*token_pieces, gains, weight, cosine, sine),
    )
    grad_pieces = spread_all(after(own_grad, token_pieces))
    keyval_other = swap_ctx(keyval)
    key_scratch = [((4, 256, 3 * TILE), BF16), ((4, 3 * TILE, 256), BF16), ((3, 256, 256), F32)]
    mixed, logs = chain.call(
        "attend",
        attend_body,
        [((row_count * 768, TILE), BF16), ((row_count * 2, 8, 256), F32)],
        (ends,),
        (query, keyval, keyval_other),
        key_scratch + [((3, 256, 256), F32)],
    )
    head_pieces = spread_all(mixed)
    output = second_full[:, :features]
    gateup = second_full[:, features : features + 2 * hidden_width]
    down = second_full[:, features + 2 * hidden_width :]
    piece_shape = ((own_rows, features), BF16)
    feed = chain.call(
        "feed",
        feed_body,
        [piece_shape] * 4
        + [
            ((count, features), BF16),
            ((count, hidden_width), BF16),
            ((count, 2 * hidden_width), BF16),
            ((count, features), BF16),
            ((own_rows, features), F32),
            ((own_rows, features), BF16),
        ],
        (ends,),
        (hidden, *head_pieces, *grad_pieces, gains, output, gateup, down),
        [((256, features), BF16), ((256, features), BF16), ((256, features), F32)],
    )
    second_grads = exchange(feed[:4])
    second, active, feed_grads, spread, middle_own, heads_own = feed[4:]
    feed_sum = chain.call(
        "feed_weights",
        feed_weights_body,
        [((features, 3 * hidden_width + features), BF16)],
        (),
        (second, feed_grads, active, spread),
        [((features, count), BF16), ((features, count), BF16)],
    )[0]
    fed = chain.call(
        "fed",
        fed_body,
        [((PARTS, own_rows, features), BF16)],
        (),
        (active, down),
        [((256, features), BF16)],
    )[0]
    sends = chain.call(
        "middle",
        middle_body,
        [((row_count * 192, TILE), BF16)] * 4
        + [((own_rows, features), F32), ((own_rows, features), BF16), ((8, features), F32)],
        (ends,),
        (*second_grads, middle_own, own_grad, gains, output),
    )
    grad_heads = exchange(sends[:4])
    grad_middle, grad_low, gain_two = sends[4:]
    grad_heads = exchange(sends[:4])
    grad_middle, grad_low, gain_two = sends[4:]
    feed_total = lax.psum_scatter(
        after(feed_sum, grad_low), ("dp", "ctx"), scatter_dimension=0, tiled=True
    ).astype(F32)
    wide_sum = chain.call(
        "output_weights",
        output_weights_body,
        [],
        (),
        (grad_low, heads_own),
        [((features, features), BF16)],
        grown=feed_sum,
    )[0]
    fed_landed = lax.all_to_all(after(fed, grad_heads), "tensor", 0, 0)
    block_output = middle_own + fed_landed.astype(F32).sum(axis=0)
    block_output = block_output.astype(BF16).reshape(tokens.shape)
    grad_query, grad_own, grad_other = chain.call(
        "attend_back",
        attend_back_body,
        [((count, 2 * TILE), BF16), ((count, 3 * TILE), F32), ((count, 3 * TILE), BF16)],
        (ends,),
        (query, keyval, keyval_other, *grad_heads, logs, cosine, sine),
        key_scratch
        + [
            ((2, 256, 2 * TILE), BF16),
            ((3, 256, 256), F32),
            ((3, 256, 256), F32),
            ((4, 256, 3 * TILE), F32),
        ],
    )
    arrived = swap_ctx(grad_other)
    wide_total = lax.psum_scatter(
        after(wide_sum, grad_other), ("dp", "ctx"), scatter_dimension=0, tiled=True
    ).astype(F32)
    feed_total = wide_total[:, : 3 * hidden_width]
    output_total = wide_total[:, 3 * hidden_width :]
    grads = chain.call(
        "first",
        first_body,
        [((count, QKV), BF16)],
        (),
        (grad_query, grad_own, arrived, cosine, sine),
    )[0]
    block_shape = (block_count, block_rows, QKV)
    first_sums = chain.call(
        "first_weights",
        first_weights_body,
        [(block_shape, F32), (block_shape, BF16)] if by_hand else [((features, QKV), BF16)],
        (),
        (normed, grads, weight, gains, gain_two),
        [((features, QKV), F32), ((features, count), BF16)],
    )
    if by_hand:
        arrived_one = swap_ctx(first_sums[1])
    spread_grads = chain.call(
        "spread_grad",
        spread_grad_body,
        [((PARTS, own_rows, features), BF16)],
        (),
        (grads, after(weight, fed_landed)),
        [((256, features), BF16)],
    )[0]
    first_grads = lax.all_to_all(spread_grads, "tensor", 0, 0)
    if by_hand:
        first_total = landed_blocks(context_sums(chain, first_sums[0], arrived_one))
    else:
        first_total = lax.psum_scatter(
            first_sums[0], ("dp", "ctx"), scatter_dimension=0, tiled=True
        ).astype(F32)
    input_grad = chain.call(
        "input",
        input_body,
        [((own_rows, features), F32)],
        (),
        (first_grads, own_tokens, grad_middle, gains),
    )[0].reshape(tokens.shape)

    output_sends = []
    for offset in range(PARTS):
        head_lanes = output_total[:, offset * TILE : (offset + 1) * TILE]
        start = PARTS * TILE + offset * HD
        output_sends.append(
            jnp.concatenate([head_lanes, output_total[:, start : start + HD]], axis=1)
        )
    output_grad = output_sends[0]
    for offset in range(1, PARTS):
        output_grad = output_grad + across(output_sends[offset].astype(BF16), offset).astype(F32)
    output_grad = output_grad.T

    gain_total = first_total[:, 3 * HD : 3 * HD + 2].T
    gain_size = block_rows // PARTS
    gain_grad = lax.dynamic_slice_in_dim(gain_total, part * gain_size, gain_size, 1)
    for offset in range(1, PARTS):
        target = jnp.bitwise_xor(part, offset)
        piece = lax.dynamic_slice_in_dim(gain_total, target * gain_size, gain_size, 1)
        gain_grad = gain_grad + across(piece, offset)

    query_grad = first_total[:, : HEADS * HD]
    key_tiles = [first_total[:, (2 + h) * TILE : (3 + h) * TILE] for h in range(HEADS)]
    keyvalue_grad = jnp.stack(
        [
            jnp.concatenate([tile[:, :HD] for tile in key_tiles], axis=1),
            jnp.concatenate([tile[:, HD:] for tile in key_tiles], axis=1),
        ]
    )
    gateup_grad = jnp.stack(
        [feed_total[:, :hidden_width], feed_total[:, hidden_width : 2 * hidden_width]]
    )
    down_grad = feed_total[:, 2 * hidden_width :].T
    return (
        block_output,
        input_grad,
        *adam_step(
            query_grad, query_master, query_moment, query_variance, WEIGHT_DECAY, LEARNING_RATE
        ),
        *adam_step(
            keyvalue_grad,
            keyvalue_master,
            keyvalue_moment,
            keyvalue_variance,
            WEIGHT_DECAY,
            LEARNING_RATE,
        ),
        *adam_step(
            output_grad, output_master, output_moment, output_variance, WEIGHT_DECAY, OUTPUT_RATE
        ),
        *adam_step(
            gateup_grad, gateup_master, gateup_moment, gateup_variance, WEIGHT_DECAY, LEARNING_RATE
        ),
        *adam_step(
            down_grad, down_master, down_moment, down_variance, WEIGHT_DECAY, LEARNING_RATE
        ),
        *adam_step(gain_grad, gain_master, gain_moment, gain_variance, 0.0, GAIN_RATE),
    )


def solution(mesh):
    hidden = P("dp", "ctx", None, "tensor", None)
    rows = P(("dp", "ctx"), "tensor")
    stacked = P(None, ("dp", "ctx"), "tensor")
    columns = P("tensor", ("dp", "ctx"))
    gain = P(None, ("dp", "ctx", "tensor"))
    return jax.shard_map(
        per_device,
        mesh=mesh,
        in_specs=(
            (hidden, hidden, P("dp", None), P("dp", None))
            + (rows,) * 4
            + (stacked,) * 4
            + (columns,) * 4
            + (stacked,) * 4
            + (columns,) * 4
            + (P(None, ("dp", "ctx")),)
            + (gain,) * 3
        ),
        out_specs=(
            (hidden, hidden)
            + (rows,) * 4
            + (stacked,) * 4
            + (columns,) * 4
            + (stacked,) * 4
            + (columns,) * 4
            + (gain,) * 4
        ),
        check_vma=False,
    )
```

```python
import functools

import jax
import jax.numpy as jnp
import numpy as np
from jax import lax
from jax.experimental import pallas as pl
from jax.experimental.pallas import tpu as pltpu
from jax.sharding import PartitionSpec as P

H = 12
HD = 64
STEP = 10
PARTS = 4
HEADS = H // PARTS
TILE = 2 * HD
QKV = 5 * TILE

EPSILON = 1e-05
BETA_ONE = 0.9
BETA_TWO = 0.95
ADAM_EPSILON = 1e-08
WEIGHT_DECAY = 0.1
LEARNING_RATE = 0.01
OUTPUT_RATE = 0.08
GAIN_RATE = 0.4
ROTARY_BASE = 10000.0
NEGATIVE = -1e30

F32 = jnp.float32
BF16 = jnp.bfloat16
VMEM_LIMIT = {}
FROM_HBM = ('prepare', 'prepare_rest')
SMEM = pl.BlockSpec(memory_space=pltpu.SMEM)
VMEM = pl.BlockSpec(memory_space=pltpu.VMEM)


def call(name, body, outs, scalars, arrays, scratch=(), grown=None):
    extra = () if grown is None else (grown,)
    out_shape = [jax.ShapeDtypeStruct(shape, dtype) for shape, dtype in outs]
    out_shape += [jax.ShapeDtypeStruct(value.shape, value.dtype) for value in extra]
    anywhere = [pl.BlockSpec(memory_space=pl.ANY) for _ in extra]
    scratch_shapes = [pltpu.VMEM(shape, dtype) for shape, dtype in scratch]
    if extra:
        scratch_shapes.append(pltpu.SemaphoreType.DMA(()))
    if name in FROM_HBM:
        arrays = [pltpu.with_memory_space_constraint(value, pltpu.HBM) for value in arrays]
    position = len(scalars) + len(arrays)
    return pl.pallas_call(
        body,
        out_shape=out_shape,
        in_specs=[SMEM] * len(scalars) + [VMEM] * len(arrays) + anywhere,
        out_specs=[VMEM] * len(outs) + anywhere,
        scratch_shapes=scratch_shapes,
        input_output_aliases={position: len(outs)} if extra else {},
        compiler_params=pltpu.CompilerParams(vmem_limit_bytes=VMEM_LIMIT.get(name, 8) << 20),
        name=name,
    )(*scalars, *arrays, *extra)


def dot(left, right):
    return lax.dot_general(left, right, (((1,), (0,)), ((), ())), preferred_element_type=F32)


def dot_nt(left, right):
    return lax.dot_general(left, right, (((1,), (1,)), ((), ())), preferred_element_type=F32)


def dot_tn(left, right):
    return lax.dot_general(left, right, (((0,), (0,)), ((), ())), preferred_element_type=F32)


def rows_at(start, size, unit):
    return pl.ds(pl.multiple_of(start, unit), size)


def lanes_of(shape):
    return lax.broadcasted_iota(jnp.int32, shape, len(shape) - 1)


def swapped(tile):
    first = (lanes_of(tile.shape) % HD) < HD // 2
    return jnp.where(first, pltpu.roll(tile, TILE - HD // 2, 1), pltpu.roll(tile, HD // 2, 1))


def root_mean(values):
    return lax.rsqrt(jnp.mean(values * values, axis=-1, keepdims=True) + EPSILON)


def prepare_body(meta, query, keyvalue, gain, first):
    rows, width = query.shape
    first[:, :width] = query[...]
    gains = jnp.concatenate([gain[...].astype(F32), jnp.zeros((HD - 2, rows), F32)], axis=0)
    first[:, width : width + HD] = gains.T.astype(BF16)
    for head in range(HEADS):
        start = (2 + head) * TILE
        lanes = slice(head * HD, (head + 1) * HD)
        first[:, start : start + TILE] = jnp.concatenate(
            [keyvalue[0, :, lanes], keyvalue[1, :, lanes]], axis=1
        )


def prepare_rest_body(meta, output, gateup, down, turned, rest):
    turned[...] = output[...].astype(F32).T.astype(BF16)
    hidden = down.shape[1]
    rest[:, :hidden] = gateup[0]
    rest[:, hidden : 2 * hidden] = gateup[1]
    rest[:, 2 * hidden :] = down[...]


def join_body(meta, p0, p1, p2, p3, out):
    for index, piece in enumerate((p0, p1, p2, p3)):
        out[:, index * TILE : (index + 1) * TILE] = piece[:, :TILE]
    for index, pair in enumerate(((p0, p1), (p2, p3))):
        start = (PARTS + index) * TILE
        out[:, start : start + TILE] = jnp.concatenate(
            [pair[0][:, TILE:], pair[1][:, TILE:]], axis=1
        )


def stack_body(meta, *refs):
    pieces, out = refs[:-1], refs[-1]
    count = len(pieces)
    for shift, piece in enumerate(pieces):
        out[lax.rem(meta[2] + count - shift, count)] = piece[...]


def assemble(meta, own, other, target, low, high):
    context = meta[1]
    count, rows, _ = own.shape
    for index in range(count):
        target[rows_at((2 * index + context) * rows, rows, 16), :] = own[index, :, low:high]
        target[rows_at((2 * index + 1 - context) * rows, rows, 16), :] = other[index, :, low:high]


def assemble_second_body(meta, wide_own, wide_other, rest_own, rest_other, out):
    split = wide_own.shape[2]
    context = meta[1]
    count, rows, _ = wide_own.shape
    for pair, lanes in (
        ((wide_own, wide_other), slice(0, split)),
        ((rest_own, rest_other), slice(split, out.shape[1])),
    ):
        for index in range(count):
            first = rows_at((2 * index + context) * rows, rows, 16)
            second = rows_at((2 * index + 1 - context) * rows, rows, 16)
            out[first, lanes] = pair[0][index]
            out[second, lanes] = pair[1][index]


def assemble_first_body(meta, own, other, weight, gains):
    assemble(meta, own, other, weight, 0, QKV)
    tile = weight[:, TILE : 2 * TILE].astype(F32)
    gains[...] = tile.T[HD : HD + 8, :]
    weight[:, TILE : 2 * TILE] = jnp.where(lanes_of(tile.shape) < HD, tile, 0.0).astype(BF16)


def project_body(
    meta, x0, x1, x2, x3, x4, gains, weight, cosine, sine, hidden, normed, query, keyval
):
    part = meta[0]
    blocks = x0.shape[0] // 64
    gain = gains[0:1, :]
    pieces = ((x0, 0, 0), (x1, 1, 0), (x2, 2, 0), (x3, 3, 0), (x4, 3, blocks // 2))
    for piece, offset, start in pieces:
        place = jnp.bitwise_xor(part, offset)

        def spread(block, carry, piece=piece, place=place, start=start):
            source = piece[rows_at(block * 64, 64, 64), :]
            values = source.astype(F32)
            target = rows_at((start + block) * 256 + place * 64, 64, 64)
            hidden[target, :] = source
            normed[target, :] = (values * root_mean(values) * gain).astype(BF16)
            return carry

        lax.fori_loop(0, piece.shape[0] // 64, spread, 0)

    def rotate(block, carry):
        rows = rows_at(block * 256, 256, 256)
        raw = dot(normed[rows, :], weight[...])
        cos, sin = cosine[rows, :], sine[rows, :]
        lower = lanes_of(cos.shape) < HD
        for index in range(5):
            tile = raw[:, index * TILE : (index + 1) * TILE]
            turned = tile * cos + swapped(tile) * sin
            lanes = slice((index - 2) * TILE, (index - 1) * TILE)
            if index < 2:
                query[rows, index * TILE : (index + 1) * TILE] = (turned * HD**-0.5).astype(BF16)
            else:
                keyval[rows, lanes] = jnp.where(lower, turned, tile).astype(BF16)
        return carry

    lax.fori_loop(0, blocks, rotate, 0)


def gather_keys(context, row, own, other, absolute):
    for side in range(2):
        rows = rows_at(row * 512 + side * 256, 256, 256)
        mine = context if side == 0 else 3 - context
        theirs = 1 - context if side == 0 else 2 + context
        absolute[mine] = own[rows, :]
        absolute[theirs] = other[rows, :]


def mask_bias(ends, row, query_quarter, key_quarter, documents):
    query_point = query_quarter * 256 + lax.broadcasted_iota(jnp.int32, (1, 256), 1)
    begin = jnp.zeros((1, 256), jnp.int32)
    for index in range(documents):
        end = ends[row, index]
        begin = jnp.where(query_point >= end, jnp.maximum(begin, end), begin)
    key_point = key_quarter * 256 + lax.broadcasted_iota(jnp.int32, (256, 256), 0)
    return jnp.where((key_point <= query_point) & (key_point >= begin), 0.0, NEGATIVE)


def query_pads(tiles):
    first, second = tiles[:, :TILE].astype(F32), tiles[:, TILE:].astype(F32)
    lower = lanes_of(first.shape) < HD
    return [
        jnp.where(lower, first, 0.0).astype(BF16),
        jnp.where(lower, pltpu.roll(first, HD, 1), 0.0).astype(BF16),
        jnp.where(lower, second, 0.0).astype(BF16),
    ]


def attend_body(meta, ends, query, own, other, mixed, logs, keys, keys_turned, bias, scores):
    context = meta[1]
    documents = ends.shape[1]

    def one(row, carry):
        gather_keys(context, row, own, other, keys)
        for quarter in range(4):
            for head in range(HEADS):
                lanes = slice(head * TILE, (head + 1) * TILE)
                keys_turned[quarter, lanes, :] = keys[quarter, :, lanes].astype(F32).T.astype(BF16)
        outs = []
        for side in range(2):
            quarter = context if side == 0 else 3 - context
            count = 2 + side
            base = 0 if side == 0 else 1 - context
            rows = rows_at(row * 512 + side * 256, 256, 256)
            for step in range(count):
                bias[step] = mask_bias(ends, meta[3] + row, quarter, base + step, documents)
            pads = query_pads(query[rows, :])
            turned = []
            for head in range(HEADS):
                lanes = slice(head * TILE, (head + 1) * TILE)
                highest = jnp.full((1, 256), NEGATIVE, F32)
                for step in range(count):
                    value = dot_nt(keys[base + step, :, lanes], pads[head]) + bias[step]
                    scores[step] = value
                    highest = jnp.maximum(highest, jnp.max(value, axis=0, keepdims=True))
                total = jnp.zeros((1, 256), F32)
                for step in range(count):
                    value = jnp.exp(scores[step] - highest)
                    scores[step] = value
                    total = total + jnp.sum(value, axis=0, keepdims=True)
                inverse = 1.0 / total
                result = jnp.zeros((TILE, 256), F32)
                for step in range(count):
                    weights = (scores[step] * inverse).astype(BF16)
                    result = result + dot(keys_turned[base + step, lanes, :], weights)
                turned.append(result[HD:, :])
                logs[2 * row + side, head : head + 1, :] = highest + jnp.log(total)
            pair = jnp.concatenate(turned[:2], axis=0)
            mixed[rows_at(row * 768 + side * 256, 256, 256), :] = pair.T.astype(BF16)
            outs.append(turned[2])
        packed = jnp.concatenate(outs, axis=0)
        mixed[rows_at(row * 768 + 512, 256, 256), :] = packed.T.astype(BF16)
        return carry

    lax.fori_loop(0, query.shape[0] // 512, one, 0)


def silu_parts(gating):
    gate = 1.0 / (1.0 + jnp.exp(-gating))
    return gate, gating * gate


def joined_heads(row, side, heads, target, lower):
    start = side * 256
    for index in range(PARTS):
        target[:, index * TILE : (index + 1) * TILE] = heads[index][start : start + 256, :]
    for index in range(2):
        tail = slice(512, 768)
        left = heads[2 * index][tail, :].astype(F32)
        right = heads[2 * index + 1][tail, :].astype(F32)
        if side == 0:
            tile = jnp.where(lower, left, pltpu.roll(right, HD, 1))
        else:
            tile = jnp.where(lower, pltpu.roll(left, HD, 1), right)
        target[:, (PARTS + index) * TILE : (PARTS + index + 1) * TILE] = tile.astype(BF16)


def feed_body(
    meta, ends, hidden, h0, h1, h2, h3, h4, c0, c1, c2, c3, c4, gains, wide,
    o0, o1, o2, o3, second, active, grads, spread, middle_own, heads_own,
    joined, block_grad, block_middle,
):
    part, context = meta[0], meta[1]
    features = hidden.shape[1]
    width = active.shape[1]
    output = wide.at[:, :features]
    gateup = wide.at[:, features : features + 2 * width]
    down = wide.at[:, features + 2 * width :]
    gain = gains[1:2, :]
    lower = lanes_of((256, TILE)) < HD
    row_count = hidden.shape[0] // 512
    for row in range(row_count):
        far = row >= row_count // 2
        shift = row_count // 2 if far else 0
        heads = [piece.at[row * 768 : row * 768 + 768, :] for piece in (h0, h1, h2)]
        start = (row - shift) * 768
        heads.append((h4 if far else h3).at[start : start + 768, :])
        for side in range(2):
            block = 2 * row + side
            rows = slice(block * 256, block * 256 + 256)
            joined_heads(row, side, heads, joined, lower)
            for offset, piece in enumerate((c0, c1, c2, c4 if far else c3)):
                place = jnp.bitwise_xor(part, offset)
                target = rows_at(block * 256 + place * 64, 64, 64)
                source = (block - 2 * shift if offset == 3 else block) * 64
                spread[target, :] = piece[source : source + 64, :]
            quarter = context if side == 0 else 3 - context
            point = quarter * 256 + lax.broadcasted_iota(jnp.int32, (256, 1), 0)
            keep = point < ends[meta[3] + row, ends.shape[1] - 1]
            out_grad = jnp.where(keep, spread[rows, :].astype(F32), 0.0).astype(BF16)
            spread[rows, :] = out_grad
            middle = hidden[rows, :].astype(F32) + dot_nt(joined[...], output[...])
            block_middle[...] = middle
            normed = (middle * root_mean(middle) * gain).astype(BF16)
            second[rows, :] = normed
            own = slice(block * 64, block * 64 + 64)
            mine = rows_at(part * 64, 64, 64)
            middle_own[own, :] = block_middle[mine, :]
            heads_own[own, :] = joined[mine, :]
            gate_up = dot(normed, gateup[...])
            gating, upward = gate_up[:, :width], gate_up[:, width:]
            grad_active = dot(out_grad, down[...])
            gate, passed = silu_parts(gating)
            active[rows, :] = (passed * upward).astype(BF16)
            grads[rows, :width] = (
                grad_active * upward * gate * (1.0 + gating * (1.0 - gate))
            ).astype(BF16)
            grads[rows, width:] = (grad_active * passed).astype(BF16)
            block_grad[...] = dot_nt(grads[rows, :], gateup[...]).astype(BF16)
            for offset, piece in enumerate((o0, o1, o2, o3)):
                place = jnp.bitwise_xor(part, offset)
                piece[own, :] = block_grad[rows_at(place * 64, 64, 64), :]


def fed_body(meta, active, wide, o0, o1, o2, o3, block_out):
    part = meta[0]
    down = wide.at[:, wide.shape[1] - active.shape[1] :]
    for block in range(active.shape[0] // 256):
        rows = slice(block * 256, block * 256 + 256)
        block_out[...] = dot_nt(active[rows, :], down[...]).astype(BF16)
        for offset, piece in enumerate((o0, o1, o2, o3)):
            place = jnp.bitwise_xor(part, offset)
            piece[block * 64 : block * 64 + 64, :] = block_out[rows_at(place * 64, 64, 64), :]


def give_rows(context, total, tile, outs, lanes):
    if len(outs) == 2:
        tile[...] = total
        split_rows(context, tile, *outs, lanes)
    else:
        outs[0][:, lanes] = total.astype(BF16)


def split_rows(context, source, keep, send, lanes):
    count, rows, _ = keep.shape
    for index in range(count):
        keep[index, :, lanes] = source[rows_at((2 * index + context) * rows, rows, 32), :]
        send[index, :, lanes] = source[
            rows_at((2 * index + 1 - context) * rows, rows, 32), :
        ].astype(BF16)


def feed_weights_body(meta, second, grads, active, spread, *refs):
    outs, (left, right, tile) = refs[:-3], refs[-3:]
    for block in range(second.shape[0] // 256):
        rows = slice(block * 256, block * 256 + 256)
        left[:, rows] = second[rows, :].T
        right[:, rows] = spread[rows, :].T
    width = active.shape[1]
    for start in range(0, 3 * width, 256):
        if start < 2 * width:
            total = dot(left[...], grads[:, start : start + 256])
        else:
            total = dot(right[...], active[:, start - 2 * width : start - 2 * width + 256])
        give_rows(meta[1], total, tile, outs, slice(start, start + 256))


def middle_body(
    meta, ends, g0, g1, g2, g3, middle_ref, out_grad_ref, gains, wide,
    s0, s1, s2, s3, grad_ref, low_ref, gain_ref,
):
    part, context = meta[0], meta[1]
    total = g0[...].astype(F32) + g1[...].astype(F32) + g2[...].astype(F32) + g3[...].astype(F32)
    middle = middle_ref[...]
    scale = root_mean(middle)
    gain = gains[1:2, :]
    keeps = []
    for block in range(middle.shape[0] // 64):
        row, side = block // 2, block % 2
        quarter = context if side == 0 else 3 - context
        point = quarter * 256 + part * 64 + lax.broadcasted_iota(jnp.int32, (64, 1), 0)
        keeps.append(point < ends[meta[3] + row, ends.shape[1] - 1])
    keep = jnp.concatenate([value.astype(F32) for value in keeps], axis=0)
    out_grad = out_grad_ref[...].astype(F32) * keep
    scaled = gain * total
    inner = jnp.mean(scaled * middle, axis=-1, keepdims=True)
    grad = out_grad + scale * scaled - middle * (scale * scale * scale * inner)
    grad_ref[...] = grad
    low = grad.astype(BF16)
    low_ref[...] = low
    gain_ref[...] = jnp.broadcast_to(
        jnp.sum(total * middle * scale, axis=0, keepdims=True), gain_ref.shape
    )
    heads = dot(low, wide[:, : low.shape[1]])
    lower = lanes_of((64, TILE)) < HD
    for offset, piece in enumerate((s0, s1, s2, s3)):
        tail = PARTS + offset // 2
        for row in range(middle.shape[0] // 128):
            rows = slice(row * 128, row * 128 + 128)
            piece[row * 192 : row * 192 + 128, :] = heads[
                rows, offset * TILE : (offset + 1) * TILE
            ].astype(BF16)
            former = heads[row * 128 : row * 128 + 64, tail * TILE : (tail + 1) * TILE]
            latter = heads[row * 128 + 64 : row * 128 + 128, tail * TILE : (tail + 1) * TILE]
            if offset % 2 == 0:
                packed = jnp.where(lower, former, pltpu.roll(latter, HD, 1))
            else:
                packed = jnp.where(lower, pltpu.roll(former, HD, 1), latter)
            piece[row * 192 + 128 : row * 192 + 192, :] = packed.astype(BF16)


def output_weights_body(meta, low, heads, *refs):
    outs, tile = refs[:-1], refs[-1]
    turned = low[...].T
    for start in range(0, heads.shape[1], 256):
        total = dot(turned, heads[:, start : start + 256])
        give_rows(meta[1], total, tile, outs, slice(start, start + 256))


def attend_back_body(
    meta, ends, query, own, other, g0, g1, g2, g3, logs, cosine, sine,
    grad_query, grad_own, grad_other, keys, keys_turned, bias, grad_heads, probs, grad_probs, sums,
):
    part, context = meta[0], meta[1]
    documents = ends.shape[1]

    def one(row, carry):
        gather_keys(context, row, own, other, keys)
        sums[...] = jnp.zeros_like(sums)
        for quarter in range(4):
            for head in range(HEADS):
                lanes = slice(head * TILE, (head + 1) * TILE)
                keys_turned[quarter, lanes, :] = keys[quarter, :, lanes].astype(F32).T.astype(BF16)
        for offset, piece in enumerate((g0, g1, g2, g3)):
            place = jnp.bitwise_xor(part, offset)
            for side in range(2):
                start = row * 192 + side * 64
                grad_heads[side, rows_at(place * 64, 64, 64), :TILE] = piece[rows_at(start, 64, 64), :]
            grad_heads[0, rows_at(place * 64, 64, 64), TILE:] = piece[
                rows_at(row * 192 + 128, 64, 64), :
            ]
        for side in range(2):
            quarter = context if side == 0 else 3 - context
            count = 2 + side
            base = 0 if side == 0 else 1 - context
            rows = rows_at(row * 512 + side * 256, 256, 256)
            for step in range(count):
                bias[step] = mask_bias(ends, meta[3] + row, quarter, base + step, documents)
            pads = query_pads(query[rows, :])
            first = grad_heads[side, :, :TILE].astype(F32)
            second = grad_heads[0, :, TILE:].astype(F32)
            upper = lanes_of(first.shape) >= HD
            tail = pltpu.roll(second, HD, 1) if side == 0 else second
            grads = [
                jnp.where(upper, pltpu.roll(first, HD, 1), 0.0).astype(BF16),
                jnp.where(upper, first, 0.0).astype(BF16),
                jnp.where(upper, tail, 0.0).astype(BF16),
            ]
            turned = []
            for head in range(HEADS):
                lanes = slice(head * TILE, (head + 1) * TILE)
                log = logs[2 * row + side, head : head + 1, :]
                inner = jnp.zeros((1, 256), F32)
                for step in range(count):
                    block = keys[base + step, :, lanes]
                    chance = jnp.exp(dot_nt(block, pads[head]) + bias[step] - log)
                    slope = dot_nt(block, grads[head])
                    probs[step] = chance
                    grad_probs[step] = slope
                    inner = inner + jnp.sum(chance * slope, axis=0, keepdims=True)
                sides = jnp.concatenate([pads[head], grads[head]], axis=0)
                result = jnp.zeros((TILE, 256), F32)
                for step in range(count):
                    chance = probs[step]
                    slope = (chance * (grad_probs[step] - inner)).astype(BF16)
                    both = jnp.concatenate([slope, chance.astype(BF16)], axis=1)
                    sums[base + step, :, lanes] += dot(both, sides)
                    result = result + dot(keys_turned[base + step, lanes, :], slope)
                turned.append(result[:HD, :])
            cos, sin = cosine[rows, :], sine[rows, :]
            turned.append(jnp.zeros((HD, 256), F32))
            for index in range(2):
                tile = jnp.concatenate(turned[2 * index : 2 * index + 2], axis=0).T * HD**-0.5
                grad_query[rows, index * TILE : (index + 1) * TILE] = (
                    tile * cos - swapped(tile) * sin
                ).astype(BF16)
        for side in range(2):
            rows = rows_at(row * 512 + side * 256, 256, 256)
            mine = context if side == 0 else 3 - context
            theirs = 1 - context if side == 0 else 2 + context
            grad_own[rows, :] = sums[mine]
            grad_other[rows, :] = sums[theirs].astype(BF16)
        return carry

    lax.fori_loop(0, query.shape[0] // 512, one, 0)


def first_body(meta, grad_query, grad_own, arrived, cosine, sine, grads):
    def one(block, carry):
        rows = rows_at(block * 256, 256, 256)
        cos, sin = cosine[rows, :], sine[rows, :]
        lower = lanes_of(cos.shape) < HD
        grads[rows, : 2 * TILE] = grad_query[rows, :]
        for index in range(HEADS):
            lanes = slice(index * TILE, (index + 1) * TILE)
            tile = grad_own[rows, lanes] + arrived[rows, lanes].astype(F32)
            turned = tile * cos - swapped(tile) * sin
            grads[rows, (2 + index) * TILE : (3 + index) * TILE] = jnp.where(
                lower, turned, tile
            ).astype(BF16)
        return carry

    lax.fori_loop(0, grad_query.shape[0] // 256, one, 0)


def spread_grad_body(meta, grads, weight, out, block_grad):
    def one(block, carry):
        rows = rows_at(block * 256, 256, 256)
        block_grad[...] = dot_nt(grads[rows, :], weight[...]).astype(BF16)
        for place in range(PARTS):
            target = rows_at(block * 64, 64, 64)
            out[place, target, :] = block_grad[place * 64 : place * 64 + 64, :]
        return carry

    lax.fori_loop(0, grads.shape[0] // 256, one, 0)


def first_weights_body(meta, normed, grads, weight, gains, gain_two, *refs):
    outs, total, turned = refs[:-2], refs[-2], refs[-1]
    turned[...] = normed[...].T
    width = total.shape[1]
    for start in range(0, width, TILE):
        lanes = slice(start, start + TILE)
        total[:, lanes] = dot(turned[...], grads[:, lanes])
    product = total[...] * weight[...].astype(F32)
    column = jnp.sum(product, axis=1, keepdims=True)
    lane = lanes_of((normed.shape[1], TILE))
    row = lax.broadcasted_iota(jnp.int32, (TILE, normed.shape[1]), 0)
    two = jnp.where(row == HD + 1, gain_two[0:1, :], 0.0)
    one = jnp.where(row == HD, 1.0 / gains[0:1, :], 0.0)
    total[:, TILE : 2 * TILE] += two.T + one.T * column
    if len(outs) == 2:
        split_rows(meta[1], total, *outs, slice(0, width))
    else:
        outs[0][...] = total[...].astype(BF16)


def input_body(meta, landed, tokens, grad_middle, gains, out):
    total = landed[0].astype(F32)
    for index in range(1, PARTS):
        total = total + landed[index].astype(F32)
    values = tokens[...].astype(F32)
    scale = root_mean(values)
    scaled = gains[0:1, :] * total
    inner = jnp.mean(scaled * values, axis=-1, keepdims=True)
    out[...] = grad_middle[...] + scale * scaled - values * (scale * scale * scale * inner)


def collect_body(meta, *refs):
    pieces, first, packed = refs[: -1 - PARTS], refs[-1 - PARTS], refs[-PARTS:]
    count = len(pieces) // 2
    total, wide = pieces[0][...].astype(F32), pieces[count][...].astype(F32)
    for index in range(1, count):
        total = total + pieces[index][...].astype(F32)
        wide = wide + pieces[count + index][...].astype(F32)
    first[...] = total
    rows, width = total.shape[0], packed[0].shape[1]
    turned = total[:, TILE : 2 * TILE].T
    gains = jnp.concatenate([turned[HD : HD + 1, :], turned[HD + 1 : HD + 2, :]], axis=1)
    high = gains.astype(BF16)
    low = (gains - high.astype(F32)).astype(BF16)
    tail = jnp.concatenate([high, low, jnp.zeros((14, 2 * rows), BF16)], axis=0)
    for offset in range(PARTS):
        start = offset * TILE
        rest = PARTS * TILE + offset * HD
        packed[offset][:rows, :TILE] = wide[:, start : start + TILE].astype(BF16)
        packed[offset][:rows, TILE:] = wide[:, rest : rest + HD].astype(BF16)
        packed[offset][rows:, :] = jnp.pad(tail, ((0, 0), (0, width - 2 * rows)))


def finish_body(meta, p0, p1, p2, p3, *refs):
    output_states, gain_states = refs[:3], refs[3:6]
    output_outs, gain_outs = refs[6:10], refs[10:]
    total = p0[...].astype(F32) + p1[...].astype(F32) + p2[...].astype(F32) + p3[...].astype(F32)
    width, rows = output_outs[0].shape
    values = adam_step(
        total[:rows, :].T, *[ref[...] for ref in output_states], WEIGHT_DECAY, OUTPUT_RATE
    )
    for out, value in zip(output_outs, values):
        out[...] = value
    gains = total[rows : rows + 1, :] + total[rows + 1 : rows + 2, :]
    size = gain_outs[0].shape[1]
    picked = []
    for index in range(2):
        kept = jnp.zeros((1, size), F32)
        for place in range(PARTS):
            start = index * rows + place * size
            kept = jnp.where(meta[0] == place, gains[:, start : start + size], kept)
        picked.append(kept)
    values = adam_step(
        jnp.concatenate(picked, axis=0), *[ref[...] for ref in gain_states], 0.0, GAIN_RATE
    )
    for out, value in zip(gain_outs, values):
        out[...] = value


def context_sum_body(meta, *refs):
    count = refs[0].shape[0]
    pairs, outs = refs[:-count], refs[-count:]
    for shift, out in enumerate(outs):
        index = lax.rem(meta[2] + shift, count)
        start = 0
        for keep, arrived in zip(pairs[::2], pairs[1::2]):
            width = keep.shape[2]
            total = keep[index] + arrived[index].astype(F32)
            out[:, start : start + width] = total.astype(out.dtype)
            start += width


def tables_body(meta, lengths, dealing, inverse, ends, cosine, sine):
    rows, documents = dealing.shape
    quarters = (meta[1], 3 - meta[1])
    for row in range(rows):
        total = jnp.int32(0)
        for index in range(documents):
            total = total + lengths[row, dealing[row, index]]
            ends[row, index] = total
    sign = jnp.where((lanes_of((1, TILE)) % HD) < HD // 2, -1.0, 1.0)

    def one(block, carry):
        row = block // 2
        quarter = jnp.where(block % 2 == 0, quarters[0], quarters[1])
        point = quarter * 256 + lax.broadcasted_iota(jnp.int32, (256, 1), 0)
        begin = jnp.zeros((256, 1), jnp.int32)
        for index in range(documents):
            end = ends[row, index]
            begin = jnp.where(point >= end, end, begin)
        phase = (point - begin).astype(F32) * inverse[...]
        target = rows_at(block * 256, 256, 256)
        cosine[target, :] = jnp.cos(phase)
        sine[target, :] = jnp.sin(phase) * sign
        return carry

    lax.fori_loop(0, 2 * rows, one, 0)


def rotary_tables(meta, lengths, dealing):
    inverse = ROTARY_BASE ** (-(np.arange(HD // 2, dtype=np.float64) * 2.0 / HD))
    inverse = np.tile(inverse, 4).astype(np.float32)[None]
    rows, documents = dealing.shape
    table = jax.ShapeDtypeStruct((rows * 512, TILE), F32)
    return pl.pallas_call(
        tables_body,
        out_shape=[jax.ShapeDtypeStruct((rows, documents), jnp.int32), table, table],
        in_specs=[SMEM, SMEM, SMEM, VMEM],
        out_specs=[SMEM, VMEM, VMEM],
        compiler_params=pltpu.CompilerParams(vmem_limit_bytes=4 << 20),
        name="tables",
    )(meta, lengths, dealing, jnp.asarray(inverse))


def adam_step(gradient, master, moment, variance, decay, rate):
    moment_new = BETA_ONE * moment + (1.0 - BETA_ONE) * gradient
    variance_new = BETA_TWO * variance + (1.0 - BETA_TWO) * gradient * gradient
    first_fix = 1.0 - BETA_ONE**STEP
    second_fix = 1.0 - BETA_TWO**STEP
    stepped = (
        moment_new / first_fix / (jnp.sqrt(variance_new / second_fix) + ADAM_EPSILON)
        + decay * master
    )
    return (gradient, master - rate * stepped, moment_new, variance_new)


def swap_ctx(value):
    return lax.ppermute(value, "ctx", [(0, 1), (1, 0)])


def across(value, offset):
    return lax.ppermute(value, "tensor", [(i, i ^ offset) for i in range(PARTS)])


def shift_dp(value, shift):
    size = lax.axis_size("dp")
    return lax.ppermute(value, "dp", [(i, (i + shift) % size) for i in range(size)])


def spread_all(value):
    return [value] + [across(value, offset) for offset in range(1, PARTS)]


def spread_in_turn(value):
    half = value.shape[0] // 2
    first, second = across(value, 1), across(value, 2)
    return [value, first, second, across(second[:half], 1), across(first[half:], 2)]


def exchange(pieces):
    return [pieces[0]] + [across(pieces[offset], offset) for offset in range(1, PARTS)]


def after(value, *others):
    return lax.optimization_barrier((value, others))[0]


class Chain:
    def __init__(self, meta):
        self.meta = meta

    def call(self, name, body, outs, scalars, arrays, scratch=(), grown=None):
        results = call(name, body, outs, (self.meta, *scalars), arrays, scratch, grown)
        self.meta = after(self.meta, results[-1])
        return results


def gather_blocks(block):
    count = lax.axis_size("dp")
    return [block] + [shift_dp(block, shift) for shift in range(1, count)]


def stack_blocks(chain, pieces):
    shape = (len(pieces), *pieces[0].shape)
    return chain.call("stack", stack_body, [(shape, BF16)], (), pieces)[0]


def context_sums(chain, *pairs):
    count, rows, _ = pairs[0].shape
    width = sum(value.shape[2] for value in pairs[::2])
    outs = [((rows, width), F32)] + [((rows, width), BF16)] * (count - 1)
    return chain.call("context_sum", context_sum_body, outs, (), pairs)


def landed_blocks(sums):
    return [sums[0]] + [shift_dp(sums[shift], shift) for shift in range(1, len(sums))]


def per_device(
    tokens,
    cotangent,
    document_lengths,
    dealing,
    query_weight,
    query_master,
    query_moment,
    query_variance,
    keyvalue_weight,
    keyvalue_master,
    keyvalue_moment,
    keyvalue_variance,
    output_weight,
    output_master,
    output_moment,
    output_variance,
    gateup_weight,
    gateup_master,
    gateup_moment,
    gateup_variance,
    down_weight,
    down_master,
    down_moment,
    down_variance,
    norm_gain,
    gain_master,
    gain_moment,
    gain_variance,
):
    features = tokens.shape[-1]
    row_count = tokens.shape[0]
    block_rows = query_weight.shape[0]
    hidden_width = down_weight.shape[0]
    block_count = lax.axis_size("dp")
    part = lax.axis_index("tensor").astype(jnp.int32)
    context = lax.axis_index("ctx").astype(jnp.int32)
    own_dp = lax.axis_index("dp").astype(jnp.int32)
    meta = jnp.stack([part, context, own_dp, jnp.int32(0)])

    chain = Chain(meta)
    own_rows = row_count * 128
    count = row_count * 512
    own_tokens = tokens.reshape(own_rows, features)
    own_grad = cotangent.reshape(own_rows, features)
    by_hand = block_rows % 32 == 0 and block_count == 4
    half = own_rows // 2
    first_block = chain.call(
        "prepare",
        prepare_body,
        [((block_rows, QKV), BF16)],
        (),
        (query_weight, keyvalue_weight, norm_gain),
    )[0]
    turned_output, rest_block = chain.call(
        "prepare_rest",
        prepare_rest_body,
        [(output_weight.shape[::-1], BF16), ((block_rows, 3 * hidden_width), BF16)],
        (),
        (output_weight, gateup_weight, down_weight.T),
    )
    ends, cosine, sine = rotary_tables(chain.meta, document_lengths, dealing)

    tokens_x, tokens_y = across(own_tokens, 1), across(own_tokens, 2)
    if by_hand:
        first_pieces = [first_block] + [shift_dp(first_block, shift) for shift in (1, 2, 3)]
    else:
        first_pieces = [lax.all_gather(first_block, ("dp", "ctx"), axis=0, tiled=True)]
    done = (tokens_x, tokens_y, first_pieces[1:], cosine)

    tokens_d = [
        across(after(tokens_y, done)[:half], 1),
        across(after(tokens_x, done)[half:], 2),
    ]
    rest_pieces = [rest_block]
    if by_hand:
        rest_pieces.append(shift_dp(after(rest_block, done), 1))
        first_own = stack_blocks(chain, after(first_pieces, done))
        weight, gains = chain.call(
            "assemble_first",
            assemble_first_body,
            [((features, QKV), BF16), ((8, features), F32)],
            (),
            (first_own, swap_ctx(first_own)),
        )
    else:
        first_full = first_pieces[0]
        gains = jnp.pad(first_full[:, 3 * HD : 3 * HD + 2].T.astype(F32), ((0, 6), (0, 0)))
        lane = jnp.arange(QKV)
        weight = jnp.where((lane >= 3 * HD) & (lane < 4 * HD), 0, first_full).astype(BF16)
    done = (tokens_d, rest_pieces[1:], weight)

    grads_x = across(after(own_grad, done), 1)
    grads_y = across(after(own_grad, done), 2)
    wide_y = across(after(turned_output, done), 2)
    if by_hand:
        rest_pieces.append(shift_dp(after(rest_block, done), 2))
    hidden, normed, query, keyval = chain.call(
        "project",
        project_body,
        [((count, features), BF16)] * 2 + [((count, 2 * TILE), BF16), ((count, 3 * TILE), BF16)],
        (),
        (
            own_tokens,
            tokens_x,
            tokens_y,
            *tokens_d,
            gains,
            after(weight, done),
            cosine,
            sine,
        ),
    )
    done = (grads_x, grads_y, wide_y, rest_pieces[1:])
    keyval_other = swap_ctx(after(keyval, done))
    wide_x = across(after(turned_output, keyval, done), 1)
    wide_d = across(after(turned_output, keyval, done), 3)
    done = (keyval_other, wide_x, wide_d)

    grads_d = [
        across(after(grads_y, done)[:half], 1),
        across(after(grads_x, done)[half:], 2),
    ]
    if by_hand:
        rest_pieces.append(shift_dp(after(rest_block, done), 3))
    key_scratch = [((4, 256, 3 * TILE), BF16), ((4, 3 * TILE, 256), BF16), ((3, 256, 256), F32)]
    mixed, logs = chain.call(
        "attend",
        attend_body,
        [((row_count * 768, TILE), BF16), ((row_count * 2, 8, 256), F32)],
        (ends,),
        (after(query, done), keyval, keyval_other),
        key_scratch + [((3, 256, 256), F32)],
    )
    done = (grads_d, rest_pieces[1:])

    heads_x = across(after(mixed, done), 1)
    heads_y = across(after(mixed, done), 2)
    wide_block = chain.call(
        "join",
        join_body,
        [((block_rows, features), BF16)],
        (),
        (turned_output, wide_x, wide_y, wide_d),
    )[0]
    if by_hand:
        wide_pieces = [wide_block] + [
            shift_dp(after(wide_block, done), shift) for shift in (1, 2, 3)
        ]
        rest_own = stack_blocks(chain, after(rest_pieces, done))
        done = (heads_x, heads_y, wide_pieces[1:], rest_own)
        rest_other = swap_ctx(after(rest_own, done))
        wide_own = stack_blocks(chain, after(wide_pieces, done))
        second_full = chain.call(
            "assemble_second",
            assemble_second_body,
            [((features, features + 3 * hidden_width), BF16)],
            (),
            (wide_own, swap_ctx(wide_own), rest_own, rest_other),
        )[0]
    else:
        done = (heads_x, heads_y)
        second_full = lax.all_gather(
            jnp.concatenate([wide_block, rest_block], axis=1), ("dp", "ctx"), axis=0, tiled=True
        )
    half_heads = mixed.shape[0] // 2
    heads_d = [
        across(after(heads_y, done)[:half_heads], 1),
        across(after(heads_x, done)[half_heads:], 2),
    ]
    piece_shape = ((own_rows, features), BF16)
    feed = chain.call(
        "feed",
        feed_body,
        [piece_shape] * 4
        + [
            ((count, features), BF16),
            ((count, hidden_width), BF16),
            ((count, 2 * hidden_width), BF16),
            ((count, features), BF16),
            ((own_rows, features), F32),
            ((own_rows, features), BF16),
        ],
        (ends,),
        (
            hidden,
            mixed,
            heads_x,
            heads_y,
            *heads_d,
            own_grad,
            grads_x,
            grads_y,
            *grads_d,
            gains,
            second_full,
        ),
        [((256, features), BF16), ((256, features), BF16), ((256, features), F32)],
    )
    second, active, feed_grads, spread, middle_own, heads_own = feed[4:]

    def block_outs(width):
        if by_hand:
            shape = (block_count, block_rows, width)
            return [(shape, F32), (shape, BF16)]
        return [((features, width), BF16)]

    second_grads = exchange(feed[:4])
    feed_sums = chain.call(
        "feed_weights",
        feed_weights_body,
        block_outs(3 * hidden_width),
        (),
        (second, feed_grads, active, spread),
        [((features, count), BF16), ((features, count), BF16), ((features, 256), F32)],
    )
    if by_hand:
        feed_parts = context_sums(chain, feed_sums[0], swap_ctx(feed_sums[1]))
    fed = chain.call(
        "fed",
        fed_body,
        [piece_shape] * 4,
        (),
        (active, second_full),
        [((256, features), BF16)],
    )
    feed_landed = []
    if by_hand:
        feed_landed = [feed_parts[0]]
        feed_landed += [shift_dp(after(feed_parts[k], fed[0]), k) for k in (1, 3)]
        middle_own = after(middle_own, feed_landed[1:])
    sends = chain.call(
        "middle",
        middle_body,
        [((row_count * 192, TILE), BF16)] * 4
        + [((own_rows, features), F32), ((own_rows, features), BF16), ((8, features), F32)],
        (ends,),
        (*second_grads, middle_own, own_grad, gains, second_full),
    )
    grad_middle, grad_low, gain_two = sends[4:]
    grad_heads = exchange(sends[:4])
    output_sums = chain.call(
        "output_weights",
        output_weights_body,
        block_outs(features),
        (),
        (grad_low, heads_own),
        [((features, 256), F32)],
    )
    done = (grad_heads,)

    fed_near = [across(after(fed[offset], done), offset) for offset in (1, 2)]
    if by_hand:
        feed_landed.append(shift_dp(after(feed_parts[2], done), 2))
        arrived_output = swap_ctx(after(output_sums[1], done))
    else:
        arrived_output = grad_low
    grad_query, grad_own, grad_other = chain.call(
        "attend_back",
        attend_back_body,
        [((count, 2 * TILE), BF16), ((count, 3 * TILE), F32), ((count, 3 * TILE), BF16)],
        (ends,),
        (query, keyval, keyval_other, *grad_heads, logs, cosine, sine),
        key_scratch
        + [
            ((2, 256, 2 * TILE), BF16),
            ((3, 256, 256), F32),
            ((3, 256, 256), F32),
            ((4, 256, 3 * TILE), F32),
        ],
    )
    done = (fed_near, arrived_output, feed_landed[3:])
    arrived = swap_ctx(after(grad_other, done))

    fed_far = across(after(fed[3], arrived), 3)
    output_landed = []
    if by_hand:
        output_parts = context_sums(chain, output_sums[0], after(arrived_output, arrived))
        output_landed = [output_parts[0]] + [shift_dp(output_parts[k], k) for k in (1, 2, 3)]
    block_output = middle_own
    for piece in (fed[0], *fed_near, fed_far):
        block_output = block_output + piece.astype(F32)
    block_output = block_output.astype(BF16).reshape(tokens.shape)
    grads = chain.call(
        "first",
        first_body,
        [((count, QKV), BF16)],
        (),
        (grad_query, grad_own, arrived, cosine, sine),
    )[0]
    first_sums = chain.call(
        "first_weights",
        first_weights_body,
        block_outs(QKV),
        (),
        (normed, grads, weight, gains, gain_two),
        [((features, QKV), F32), ((features, count), BF16)],
    )
    spread_grads = chain.call(
        "spread_grad",
        spread_grad_body,
        [((PARTS, own_rows, features), BF16)],
        (),
        (grads, weight),
        [((256, features), BF16)],
    )[0]
    done = (fed_far, output_landed[1:])
    arrived_first = swap_ctx(after(first_sums[1], spread_grads, done)) if by_hand else grads
    first_grads = lax.all_to_all(after(spread_grads, done), "tensor", 0, 0)
    if by_hand:
        feed_total = feed_landed[0]
        for piece in feed_landed[1:]:
            feed_total = feed_total + piece.astype(F32)
        last_parts = context_sums(chain, first_sums[0], arrived_first)
        last_landed = [last_parts[0]] + [shift_dp(last_parts[k], k) for k in (1, 2, 3)]
    else:
        scatter = functools.partial(
            lax.psum_scatter, axis_name=("dp", "ctx"), scatter_dimension=0, tiled=True
        )
        last_landed = [scatter(first_sums[0])]
        output_landed = [scatter(output_sums[0])]
        feed_total = scatter(feed_sums[0]).astype(F32)
    packed_shape = (block_rows + 16, HEADS * HD)
    first_total, *packed = chain.call(
        "collect",
        collect_body,
        [((block_rows, QKV), F32)] + [(packed_shape, BF16)] * PARTS,
        (),
        (*last_landed, *output_landed),
    )
    packed = exchange(packed)
    input_grad = chain.call(
        "input",
        input_body,
        [((own_rows, features), F32)],
        (),
        (first_grads, own_tokens, grad_middle, gains),
    )[0].reshape(tokens.shape)
    output_results = chain.call(
        "finish",
        finish_body,
        [(output_weight.shape, F32)] * 4 + [(gain_master.shape, F32)] * 4,
        (),
        (
            *packed,
            output_master,
            output_moment,
            output_variance,
            gain_master,
            gain_moment,
            gain_variance,
        ),
    )

    query_grad = first_total[:, : HEADS * HD]
    key_tiles = [first_total[:, (2 + h) * TILE : (3 + h) * TILE] for h in range(HEADS)]
    keyvalue_grad = jnp.stack(
        [
            jnp.concatenate([tile[:, :HD] for tile in key_tiles], axis=1),
            jnp.concatenate([tile[:, HD:] for tile in key_tiles], axis=1),
        ]
    )
    gateup_grad = jnp.stack(
        [feed_total[:, :hidden_width], feed_total[:, hidden_width : 2 * hidden_width]]
    )
    down_grad = feed_total[:, 2 * hidden_width :].T
    return (
        block_output,
        input_grad,
        *adam_step(
            query_grad, query_master, query_moment, query_variance, WEIGHT_DECAY, LEARNING_RATE
        ),
        *adam_step(
            keyvalue_grad,
            keyvalue_master,
            keyvalue_moment,
            keyvalue_variance,
            WEIGHT_DECAY,
            LEARNING_RATE,
        ),
        *output_results[:4],
        *adam_step(
            gateup_grad, gateup_master, gateup_moment, gateup_variance, WEIGHT_DECAY, LEARNING_RATE
        ),
        *adam_step(
            down_grad, down_master, down_moment, down_variance, WEIGHT_DECAY, LEARNING_RATE
        ),
        *output_results[4:],
    )


def solution(mesh):
    hidden = P("dp", "ctx", None, "tensor", None)
    rows = P(("dp", "ctx"), "tensor")
    stacked = P(None, ("dp", "ctx"), "tensor")
    columns = P("tensor", ("dp", "ctx"))
    gain = P(None, ("dp", "ctx", "tensor"))
    return jax.shard_map(
        per_device,
        mesh=mesh,
        in_specs=(
            (hidden, hidden, P("dp", None), P("dp", None))
            + (rows,) * 4
            + (stacked,) * 4
            + (columns,) * 4
            + (stacked,) * 4
            + (columns,) * 4
            + (P(None, ("dp", "ctx")),)
            + (gain,) * 3
        ),
        out_specs=(
            (hidden, hidden)
            + (rows,) * 4
            + (stacked,) * 4
            + (columns,) * 4
            + (stacked,) * 4
            + (columns,) * 4
            + (gain,) * 4
        ),
        check_vma=False,
    )
```

```python
import functools

import jax
import jax.numpy as jnp
import numpy as np
from jax import lax
from jax.experimental import pallas as pl
from jax.experimental.pallas import tpu as pltpu
from jax.sharding import PartitionSpec as P

H = 12
HD = 64
STEP = 10
PARTS = 4
HEADS = H // PARTS
TILE = 2 * HD
QKV = 5 * TILE

EPSILON = 1e-05
BETA_ONE = 0.9
BETA_TWO = 0.95
ADAM_EPSILON = 1e-08
WEIGHT_DECAY = 0.1
LEARNING_RATE = 0.01
OUTPUT_RATE = 0.08
GAIN_RATE = 0.4
ROTARY_BASE = 10000.0
NEGATIVE = -1e30

F32 = jnp.float32
BF16 = jnp.bfloat16
VMEM_LIMIT = {}
FROM_HBM = ('prepare',)
SMEM = pl.BlockSpec(memory_space=pltpu.SMEM)
VMEM = pl.BlockSpec(memory_space=pltpu.VMEM)


def call(name, body, outs, scalars, arrays, scratch=(), grown=None):
    extra = () if grown is None else (grown,)
    out_shape = [jax.ShapeDtypeStruct(shape, dtype) for shape, dtype in outs]
    out_shape += [jax.ShapeDtypeStruct(value.shape, value.dtype) for value in extra]
    anywhere = [pl.BlockSpec(memory_space=pl.ANY) for _ in extra]
    scratch_shapes = [pltpu.VMEM(shape, dtype) for shape, dtype in scratch]
    if extra:
        scratch_shapes.append(pltpu.SemaphoreType.DMA(()))
    if name in FROM_HBM:
        arrays = [pltpu.with_memory_space_constraint(value, pltpu.HBM) for value in arrays]
    position = len(scalars) + len(arrays)
    return pl.pallas_call(
        body,
        out_shape=out_shape,
        in_specs=[SMEM] * len(scalars) + [VMEM] * len(arrays) + anywhere,
        out_specs=[VMEM] * len(outs) + anywhere,
        scratch_shapes=scratch_shapes,
        input_output_aliases={position: len(outs)} if extra else {},
        compiler_params=pltpu.CompilerParams(vmem_limit_bytes=VMEM_LIMIT.get(name, 8) << 20),
        name=name,
    )(*scalars, *arrays, *extra)


def dot(left, right):
    return lax.dot_general(left, right, (((1,), (0,)), ((), ())), preferred_element_type=F32)


def dot_nt(left, right):
    return lax.dot_general(left, right, (((1,), (1,)), ((), ())), preferred_element_type=F32)


def dot_tn(left, right):
    return lax.dot_general(left, right, (((0,), (0,)), ((), ())), preferred_element_type=F32)


def rows_at(start, size, unit):
    return pl.ds(pl.multiple_of(start, unit), size)


def lanes_of(shape):
    return lax.broadcasted_iota(jnp.int32, shape, len(shape) - 1)


def swapped(tile):
    first = (lanes_of(tile.shape) % HD) < HD // 2
    return jnp.where(first, pltpu.roll(tile, TILE - HD // 2, 1), pltpu.roll(tile, HD // 2, 1))


def root_mean(values):
    return lax.rsqrt(jnp.mean(values * values, axis=-1, keepdims=True) + EPSILON)


def wide_places(rows):
    places = []
    for index in range(0, -(-rows // 32)):
        size = min(32, rows - index * 32)
        source = slice(index * 32, index * 32 + size)
        tail = (3 + index // 2) * TILE + (index % 2) * HD
        places.append((source, size, index * TILE, tail))
    return places


def prepare_body(meta, query, keyvalue, gain, output, tokens, first, payload):
    rows, width = query.shape
    first[:, :width] = query[...]
    gains = jnp.concatenate([gain[...].astype(F32), jnp.zeros((HD - 2, rows), F32)], axis=0)
    first[:, width : width + HD] = gains.T.astype(BF16)
    for head in range(HEADS):
        start = (2 + head) * TILE
        lanes = slice(head * HD, (head + 1) * HD)
        first[:, start : start + TILE] = jnp.concatenate(
            [keyvalue[0, :, lanes], keyvalue[1, :, lanes]], axis=1
        )
    count = tokens.shape[0]
    payload[:count, :] = tokens[...]
    payload[count:, :] = jnp.zeros((32, tokens.shape[1]), BF16)
    turned = output[...].astype(F32).T.astype(BF16)
    for source, size, head, tail in wide_places(rows):
        payload[count : count + size, head : head + TILE] = turned[source, :TILE]
        payload[count : count + size, tail : tail + HD] = turned[source, TILE:]


def join_body(meta, p0, p1, p2, p3, gateup, down, out):
    rows, hidden = down.shape
    for source, size, head, tail in wide_places(rows):
        for index, piece in enumerate((p0, p1, p2, p3)):
            start = piece.shape[0] - 32
            lanes = slice(index * TILE, (index + 1) * TILE)
            out[source, lanes] = piece[start : start + size, head : head + TILE]
            rest = PARTS * TILE + index * HD
            out[source, rest : rest + HD] = piece[start : start + size, tail : tail + HD]
    width = PARTS * (TILE + HD)
    out[:, width : width + hidden] = gateup[0]
    out[:, width + hidden : width + 2 * hidden] = gateup[1]
    out[:, width + 2 * hidden :] = down[...]


def stack_body(meta, *refs):
    count = next(k for k in range(1, len(refs)) if refs[k].ndim == 3)
    pieces, outs = refs[:count], refs[count:]
    size = outs[0].shape[0]
    for shift, piece in enumerate(pieces):
        index = lax.rem(meta[2] + count - shift, count)
        for number, out in enumerate(outs):
            if len(outs) == 1:
                out[index] = piece[...]
            else:

                @pl.when(index // size == number)
                def _(out=out, piece=piece, index=index):
                    out[lax.rem(index, size)] = piece[...]


def assemble(meta, own, other, target, low, high, first=0):
    context = meta[1]
    count, rows, _ = own.shape
    for index in range(count):
        start = 2 * (first + index)
        target[rows_at((start + context) * rows, rows, 16), :] = own[index, :, low:high]
        target[rows_at((start + 1 - context) * rows, rows, 16), :] = other[index, :, low:high]


def assemble_second_body(meta, own, other, out):
    assemble(meta, own, other, out, 0, out.shape[1])


def assemble_first_body(meta, *refs):
    *parts, weight, gains = refs
    half = len(parts) // 2
    first = 0
    for own, other in zip(parts[:half], parts[half:]):
        assemble(meta, own, other, weight, 0, QKV, first)
        first += own.shape[0]
    tile = weight[:, TILE : 2 * TILE].astype(F32)
    gains[...] = tile.T[HD : HD + 8, :]
    weight[:, TILE : 2 * TILE] = jnp.where(lanes_of(tile.shape) < HD, tile, 0.0).astype(BF16)


def project_body(meta, x0, x1, x2, x3, gains, weight, cosine, sine, hidden, normed, query, keyval):
    part = meta[0]
    blocks = hidden.shape[0] // 256
    gain = gains[0:1, :]
    for offset, piece in enumerate((x0, x1, x2, x3)):
        place = jnp.bitwise_xor(part, offset)

        def spread(block, carry, piece=piece, place=place):
            source = piece[rows_at(block * 64, 64, 64), :]
            values = source.astype(F32)
            target = rows_at(block * 256 + place * 64, 64, 64)
            hidden[target, :] = source
            normed[target, :] = (values * root_mean(values) * gain).astype(BF16)
            return carry

        lax.fori_loop(0, blocks, spread, 0)

    def rotate(block, carry):
        rows = rows_at(block * 256, 256, 256)
        raw = dot(normed[rows, :], weight[...])
        cos, sin = cosine[rows, :], sine[rows, :]
        lower = lanes_of(cos.shape) < HD
        for index in range(5):
            tile = raw[:, index * TILE : (index + 1) * TILE]
            turned = tile * cos + swapped(tile) * sin
            lanes = slice((index - 2) * TILE, (index - 1) * TILE)
            if index < 2:
                query[rows, index * TILE : (index + 1) * TILE] = (turned * HD**-0.5).astype(BF16)
            else:
                keyval[rows, lanes] = jnp.where(lower, turned, tile).astype(BF16)
        return carry

    lax.fori_loop(0, blocks, rotate, 0)


def gather_keys(context, row, own, other, absolute):
    for side in range(2):
        rows = rows_at(row * 512 + side * 256, 256, 256)
        mine = context if side == 0 else 3 - context
        theirs = 1 - context if side == 0 else 2 + context
        absolute[mine] = own[rows, :]
        absolute[theirs] = other[rows, :]


def mask_bias(ends, row, query_quarter, key_quarter, documents):
    query_point = query_quarter * 256 + lax.broadcasted_iota(jnp.int32, (1, 256), 1)
    begin = jnp.zeros((1, 256), jnp.int32)
    for index in range(documents):
        end = ends[row, index]
        begin = jnp.where(query_point >= end, jnp.maximum(begin, end), begin)
    key_point = key_quarter * 256 + lax.broadcasted_iota(jnp.int32, (256, 256), 0)
    return jnp.where((key_point <= query_point) & (key_point >= begin), 0.0, NEGATIVE)


def query_pads(tiles):
    first, second = tiles[:, :TILE].astype(F32), tiles[:, TILE:].astype(F32)
    lower = lanes_of(first.shape) < HD
    return [
        jnp.where(lower, first, 0.0).astype(BF16),
        jnp.where(lower, pltpu.roll(first, HD, 1), 0.0).astype(BF16),
        jnp.where(lower, second, 0.0).astype(BF16),
    ]


def attend_body(meta, ends, query, own, other, mixed, logs, keys, keys_turned, bias, scores):
    context = meta[1]
    documents = ends.shape[1]

    def one(row, carry):
        gather_keys(context, row, own, other, keys)
        for quarter in range(4):
            for head in range(HEADS):
                lanes = slice(head * TILE, (head + 1) * TILE)
                keys_turned[quarter, lanes, :] = keys[quarter, :, lanes].astype(F32).T.astype(BF16)
        outs = []
        for side in range(2):
            quarter = context if side == 0 else 3 - context
            count = 2 + side
            base = 0 if side == 0 else 1 - context
            rows = rows_at(row * 512 + side * 256, 256, 256)
            for step in range(count):
                bias[step] = mask_bias(ends, meta[3] + row, quarter, base + step, documents)
            pads = query_pads(query[rows, :])
            turned = []
            for head in range(HEADS):
                lanes = slice(head * TILE, (head + 1) * TILE)
                highest = jnp.full((1, 256), NEGATIVE, F32)
                for step in range(count):
                    value = dot_nt(keys[base + step, :, lanes], pads[head]) + bias[step]
                    scores[step] = value
                    highest = jnp.maximum(highest, jnp.max(value, axis=0, keepdims=True))
                total = jnp.zeros((1, 256), F32)
                for step in range(count):
                    value = jnp.exp(scores[step] - highest)
                    scores[step] = value
                    total = total + jnp.sum(value, axis=0, keepdims=True)
                inverse = 1.0 / total
                result = jnp.zeros((TILE, 256), F32)
                for step in range(count):
                    weights = (scores[step] * inverse).astype(BF16)
                    result = result + dot(keys_turned[base + step, lanes, :], weights)
                turned.append(result[HD:, :])
                logs[2 * row + side, head : head + 1, :] = highest + jnp.log(total)
            pair = jnp.concatenate(turned[:2], axis=0)
            mixed[rows_at(row * 768 + side * 256, 256, 256), :] = pair.T.astype(BF16)
            outs.append(turned[2])
        packed = jnp.concatenate(outs, axis=0)
        mixed[rows_at(row * 768 + 512, 256, 256), :] = packed.T.astype(BF16)
        return carry

    lax.fori_loop(0, query.shape[0] // 512, one, 0)


def silu_parts(gating):
    gate = 1.0 / (1.0 + jnp.exp(-gating))
    return gate, gating * gate


def joined_heads(row, side, heads, target, lower):
    start = side * 256
    for index in range(PARTS):
        target[:, index * TILE : (index + 1) * TILE] = heads[index][start : start + 256, :]
    for index in range(2):
        tail = slice(512, 768)
        left = heads[2 * index][tail, :].astype(F32)
        right = heads[2 * index + 1][tail, :].astype(F32)
        if side == 0:
            tile = jnp.where(lower, left, pltpu.roll(right, HD, 1))
        else:
            tile = jnp.where(lower, pltpu.roll(left, HD, 1), right)
        target[:, (PARTS + index) * TILE : (PARTS + index + 1) * TILE] = tile.astype(BF16)


def feed_body(
    meta, ends, hidden, h0, h1, h2, h3, c0, c1, c2, c3, c4, gains, wide,
    o0, o1, o2, o3, second, active, grads, spread, middle_own, heads_own,
    joined, block_grad, block_middle,
):
    part, context = meta[0], meta[1]
    features = hidden.shape[1]
    width = active.shape[1]
    output = wide.at[:, :features]
    gateup = wide.at[:, features : features + 2 * width]
    down = wide.at[:, features + 2 * width :]
    gain = gains[1:2, :]
    lower = lanes_of((256, TILE)) < HD
    row_count = hidden.shape[0] // 512
    for row in range(row_count):
        far = row >= row_count // 2
        shift = row_count // 2 if far else 0
        heads = [piece.at[row * 768 : row * 768 + 768, :] for piece in (h0, h1, h2, h3)]
        for side in range(2):
            block = 2 * row + side
            rows = slice(block * 256, block * 256 + 256)
            joined_heads(row, side, heads, joined, lower)
            for offset, piece in enumerate((c0, c1, c2, c4 if far else c3)):
                place = jnp.bitwise_xor(part, offset)
                target = rows_at(block * 256 + place * 64, 64, 64)
                source = (block - 2 * shift if offset == 3 else block) * 64
                spread[target, :] = piece[source : source + 64, :]
            quarter = context if side == 0 else 3 - context
            point = quarter * 256 + lax.broadcasted_iota(jnp.int32, (256, 1), 0)
            keep = point < ends[meta[3] + row, ends.shape[1] - 1]
            out_grad = jnp.where(keep, spread[rows, :].astype(F32), 0.0).astype(BF16)
            spread[rows, :] = out_grad
            middle = hidden[rows, :].astype(F32) + dot_nt(joined[...], output[...])
            block_middle[...] = middle
            normed = (middle * root_mean(middle) * gain).astype(BF16)
            second[rows, :] = normed
            own = slice(block * 64, block * 64 + 64)
            mine = rows_at(part * 64, 64, 64)
            middle_own[own, :] = block_middle[mine, :]
            heads_own[own, :] = joined[mine, :]
            gate_up = dot(normed, gateup[...])
            gating, upward = gate_up[:, :width], gate_up[:, width:]
            grad_active = dot(out_grad, down[...])
            gate, passed = silu_parts(gating)
            active[rows, :] = (passed * upward).astype(BF16)
            grads[rows, :width] = (
                grad_active * upward * gate * (1.0 + gating * (1.0 - gate))
            ).astype(BF16)
            grads[rows, width:] = (grad_active * passed).astype(BF16)
            block_grad[...] = dot_nt(grads[rows, :], gateup[...]).astype(BF16)
            for offset, piece in enumerate((o0, o1, o2, o3)):
                place = jnp.bitwise_xor(part, offset)
                piece[own, :] = block_grad[rows_at(place * 64, 64, 64), :]


def fed_body(meta, active, wide, o0, o1, o2, o3, block_out):
    part = meta[0]
    down = wide.at[:, wide.shape[1] - active.shape[1] :]
    for block in range(active.shape[0] // 256):
        rows = slice(block * 256, block * 256 + 256)
        block_out[...] = dot_nt(active[rows, :], down[...]).astype(BF16)
        for offset, piece in enumerate((o0, o1, o2, o3)):
            place = jnp.bitwise_xor(part, offset)
            piece[block * 64 : block * 64 + 64, :] = block_out[rows_at(place * 64, 64, 64), :]


def give_rows(context, total, tile, outs, lanes):
    if len(outs) == 2:
        tile[...] = total
        split_rows(context, tile, *outs, lanes)
    else:
        outs[0][:, lanes] = total.astype(BF16)


def split_rows(context, source, keep, send, lanes):
    count, rows, _ = keep.shape
    for index in range(count):
        keep[index, :, lanes] = source[rows_at((2 * index + context) * rows, rows, 32), :]
        send[index, :, lanes] = source[
            rows_at((2 * index + 1 - context) * rows, rows, 32), :
        ].astype(BF16)


def feed_weights_body(meta, second, grads, active, spread, *refs):
    outs, (left, right, tile) = refs[:-3], refs[-3:]
    for block in range(second.shape[0] // 256):
        rows = slice(block * 256, block * 256 + 256)
        left[:, rows] = second[rows, :].T
        right[:, rows] = spread[rows, :].T
    width = active.shape[1]
    for start in range(0, 3 * width, 256):
        if start < 2 * width:
            total = dot(left[...], grads[:, start : start + 256])
        else:
            total = dot(right[...], active[:, start - 2 * width : start - 2 * width + 256])
        give_rows(meta[1], total, tile, outs, slice(start, start + 256))


def middle_body(
    meta, ends, g0, g1, g2, g3, middle_ref, out_grad_ref, gains, wide,
    s0, s1, s2, s3, grad_ref, low_ref, gain_ref,
):
    part, context = meta[0], meta[1]
    total = g0[...].astype(F32) + g1[...].astype(F32) + g2[...].astype(F32) + g3[...].astype(F32)
    middle = middle_ref[...]
    scale = root_mean(middle)
    gain = gains[1:2, :]
    keeps = []
    for block in range(middle.shape[0] // 64):
        row, side = block // 2, block % 2
        quarter = context if side == 0 else 3 - context
        point = quarter * 256 + part * 64 + lax.broadcasted_iota(jnp.int32, (64, 1), 0)
        keeps.append(point < ends[meta[3] + row, ends.shape[1] - 1])
    keep = jnp.concatenate([value.astype(F32) for value in keeps], axis=0)
    out_grad = out_grad_ref[...].astype(F32) * keep
    scaled = gain * total
    inner = jnp.mean(scaled * middle, axis=-1, keepdims=True)
    grad = out_grad + scale * scaled - middle * (scale * scale * scale * inner)
    grad_ref[...] = grad
    low = grad.astype(BF16)
    low_ref[...] = low
    gain_ref[...] = jnp.broadcast_to(
        jnp.sum(total * middle * scale, axis=0, keepdims=True), gain_ref.shape
    )
    heads = dot(low, wide[:, : low.shape[1]])
    lower = lanes_of((64, TILE)) < HD
    for offset, piece in enumerate((s0, s1, s2, s3)):
        tail = PARTS + offset // 2
        for row in range(middle.shape[0] // 128):
            rows = slice(row * 128, row * 128 + 128)
            piece[row * 192 : row * 192 + 128, :] = heads[
                rows, offset * TILE : (offset + 1) * TILE
            ].astype(BF16)
            former = heads[row * 128 : row * 128 + 64, tail * TILE : (tail + 1) * TILE]
            latter = heads[row * 128 + 64 : row * 128 + 128, tail * TILE : (tail + 1) * TILE]
            if offset % 2 == 0:
                packed = jnp.where(lower, former, pltpu.roll(latter, HD, 1))
            else:
                packed = jnp.where(lower, pltpu.roll(former, HD, 1), latter)
            piece[row * 192 + 128 : row * 192 + 192, :] = packed.astype(BF16)


def output_weights_body(meta, low, heads, *refs):
    outs, tile = refs[:-1], refs[-1]
    turned = low[...].T
    for start in range(0, heads.shape[1], 256):
        total = dot(turned, heads[:, start : start + 256])
        give_rows(meta[1], total, tile, outs, slice(start, start + 256))


def attend_back_body(
    meta, ends, query, own, other, g0, g1, g2, g3, logs, cosine, sine,
    grad_query, grad_own, grad_other, keys, keys_turned, bias, grad_heads, probs, grad_probs, sums,
):
    part, context = meta[0], meta[1]
    documents = ends.shape[1]

    def one(row, carry):
        gather_keys(context, row, own, other, keys)
        sums[...] = jnp.zeros_like(sums)
        for quarter in range(4):
            for head in range(HEADS):
                lanes = slice(head * TILE, (head + 1) * TILE)
                keys_turned[quarter, lanes, :] = keys[quarter, :, lanes].astype(F32).T.astype(BF16)
        for offset, piece in enumerate((g0, g1, g2, g3)):
            place = jnp.bitwise_xor(part, offset)
            for side in range(2):
                start = row * 192 + side * 64
                grad_heads[side, rows_at(place * 64, 64, 64), :TILE] = piece[rows_at(start, 64, 64), :]
            grad_heads[0, rows_at(place * 64, 64, 64), TILE:] = piece[
                rows_at(row * 192 + 128, 64, 64), :
            ]
        for side in range(2):
            quarter = context if side == 0 else 3 - context
            count = 2 + side
            base = 0 if side == 0 else 1 - context
            rows = rows_at(row * 512 + side * 256, 256, 256)
            for step in range(count):
                bias[step] = mask_bias(ends, meta[3] + row, quarter, base + step, documents)
            pads = query_pads(query[rows, :])
            first = grad_heads[side, :, :TILE].astype(F32)
            second = grad_heads[0, :, TILE:].astype(F32)
            upper = lanes_of(first.shape) >= HD
            tail = pltpu.roll(second, HD, 1) if side == 0 else second
            grads = [
                jnp.where(upper, pltpu.roll(first, HD, 1), 0.0).astype(BF16),
                jnp.where(upper, first, 0.0).astype(BF16),
                jnp.where(upper, tail, 0.0).astype(BF16),
            ]
            turned = []
            for head in range(HEADS):
                lanes = slice(head * TILE, (head + 1) * TILE)
                log = logs[2 * row + side, head : head + 1, :]
                inner = jnp.zeros((1, 256), F32)
                for step in range(count):
                    block = keys[base + step, :, lanes]
                    chance = jnp.exp(dot_nt(block, pads[head]) + bias[step] - log)
                    slope = dot_nt(block, grads[head])
                    probs[step] = chance
                    grad_probs[step] = slope
                    inner = inner + jnp.sum(chance * slope, axis=0, keepdims=True)
                sides = jnp.concatenate([pads[head], grads[head]], axis=0)
                result = jnp.zeros((TILE, 256), F32)
                for step in range(count):
                    chance = probs[step]
                    slope = (chance * (grad_probs[step] - inner)).astype(BF16)
                    both = jnp.concatenate([slope, chance.astype(BF16)], axis=1)
                    sums[base + step, :, lanes] += dot(both, sides)
                    result = result + dot(keys_turned[base + step, lanes, :], slope)
                turned.append(result[:HD, :])
            cos, sin = cosine[rows, :], sine[rows, :]
            turned.append(jnp.zeros((HD, 256), F32))
            for index in range(2):
                tile = jnp.concatenate(turned[2 * index : 2 * index + 2], axis=0).T * HD**-0.5
                grad_query[rows, index * TILE : (index + 1) * TILE] = (
                    tile * cos - swapped(tile) * sin
                ).astype(BF16)
        for side in range(2):
            rows = rows_at(row * 512 + side * 256, 256, 256)
            mine = context if side == 0 else 3 - context
            theirs = 1 - context if side == 0 else 2 + context
            grad_own[rows, :] = sums[mine]
            grad_other[rows, :] = sums[theirs].astype(BF16)
        return carry

    lax.fori_loop(0, query.shape[0] // 512, one, 0)


def first_body(meta, grad_query, grad_own, arrived, cosine, sine, grads):
    def one(block, carry):
        rows = rows_at(block * 256, 256, 256)
        cos, sin = cosine[rows, :], sine[rows, :]
        lower = lanes_of(cos.shape) < HD
        grads[rows, : 2 * TILE] = grad_query[rows, :]
        for index in range(HEADS):
            lanes = slice(index * TILE, (index + 1) * TILE)
            tile = grad_own[rows, lanes] + arrived[rows, lanes].astype(F32)
            turned = tile * cos - swapped(tile) * sin
            grads[rows, (2 + index) * TILE : (3 + index) * TILE] = jnp.where(
                lower, turned, tile
            ).astype(BF16)
        return carry

    lax.fori_loop(0, grad_query.shape[0] // 256, one, 0)


def spread_grad_body(meta, grads, weight, o0, o1, o2, o3, turned, block_grad):
    part = meta[0]
    turned[...] = weight[...].T
    for block in range(grads.shape[0] // 256):
        rows = slice(block * 256, block * 256 + 256)
        block_grad[...] = dot(grads[rows, :], turned[...]).astype(BF16)
        for offset, piece in enumerate((o0, o1, o2, o3)):
            place = jnp.bitwise_xor(part, offset)
            piece[block * 64 : block * 64 + 64, :] = block_grad[rows_at(place * 64, 64, 64), :]


def first_weights_body(meta, normed, grads, weight, gains, gain_two, *refs):
    outs, total, turned = refs[:-2], refs[-2], refs[-1]
    turned[...] = normed[...].T
    width = total.shape[1]
    for start, size in ((0, 256), (256, 384)):
        lanes = slice(start, start + size)
        total[:, lanes] = dot(turned[...], grads[:, lanes])
    product = total[...] * weight[...].astype(F32)
    column = jnp.sum(product, axis=1, keepdims=True)
    lane = lanes_of((normed.shape[1], TILE))
    row = lax.broadcasted_iota(jnp.int32, (TILE, normed.shape[1]), 0)
    two = jnp.where(row == HD + 1, gain_two[0:1, :], 0.0)
    one = jnp.where(row == HD, 1.0 / gains[0:1, :], 0.0)
    total[:, TILE : 2 * TILE] += two.T + one.T * column
    if len(outs) == 2:
        split_rows(meta[1], total, *outs, slice(0, width))
    else:
        outs[0][...] = total[...].astype(BF16)


def input_body(meta, g0, g1, g2, g3, tokens, grad_middle, gains, out):
    total = g0[...].astype(F32)
    for piece in (g1, g2, g3):
        total = total + piece[...].astype(F32)
    values = tokens[...].astype(F32)
    scale = root_mean(values)
    scaled = gains[0:1, :] * total
    inner = jnp.mean(scaled * values, axis=-1, keepdims=True)
    out[...] = grad_middle[...] + scale * scaled - values * (scale * scale * scale * inner)


def collect_body(meta, *refs):
    pieces, first, packed = refs[: -1 - PARTS], refs[-1 - PARTS], refs[-PARTS:]
    total, wide = None, None
    for piece in pieces:
        value = piece[...].astype(F32)
        if value.shape[1] != H * HD:
            total = value[:, :QKV] if total is None else total + value[:, :QKV]
            value = value[:, QKV:]
        if value.shape[1]:
            wide = value if wide is None else wide + value
    first[...] = total
    rows, width = total.shape[0], packed[0].shape[1]
    turned = total[:, TILE : 2 * TILE].T
    gains = jnp.concatenate([turned[HD : HD + 1, :], turned[HD + 1 : HD + 2, :]], axis=1)
    high = gains.astype(BF16)
    low = (gains - high.astype(F32)).astype(BF16)
    tail = jnp.concatenate([high, low, jnp.zeros((14, 2 * rows), BF16)], axis=0)
    for offset in range(PARTS):
        start = offset * TILE
        rest = PARTS * TILE + offset * HD
        packed[offset][:rows, :TILE] = wide[:, start : start + TILE].astype(BF16)
        packed[offset][:rows, TILE:] = wide[:, rest : rest + HD].astype(BF16)
        packed[offset][rows:, :] = jnp.pad(tail, ((0, 0), (0, width - 2 * rows)))


def finish_body(meta, p0, p1, p2, p3, *refs):
    output_states, gain_states = refs[:3], refs[3:6]
    output_outs, gain_outs = refs[6:10], refs[10:]
    total = p0[...].astype(F32) + p1[...].astype(F32) + p2[...].astype(F32) + p3[...].astype(F32)
    width, rows = output_outs[0].shape
    values = adam_step(
        total[:rows, :].T, *[ref[...] for ref in output_states], WEIGHT_DECAY, OUTPUT_RATE
    )
    for out, value in zip(output_outs, values):
        out[...] = value
    gains = total[rows : rows + 1, :] + total[rows + 1 : rows + 2, :]
    size = gain_outs[0].shape[1]
    picked = []
    for index in range(2):
        kept = jnp.zeros((1, size), F32)
        for place in range(PARTS):
            start = index * rows + place * size
            kept = jnp.where(meta[0] == place, gains[:, start : start + size], kept)
        picked.append(kept)
    values = adam_step(
        jnp.concatenate(picked, axis=0), *[ref[...] for ref in gain_states], 0.0, GAIN_RATE
    )
    for out, value in zip(gain_outs, values):
        out[...] = value


def context_sum_body(offsets, meta, *refs):
    pairs, outs = refs[: -len(offsets)], refs[-len(offsets) :]
    for offset, out in zip(offsets, outs):
        index = lax.rem(meta[2] + offset, pairs[0].shape[0])
        start = 0
        for keep, arrived in zip(pairs[::2], pairs[1::2]):
            width = keep.shape[2]
            if start + width > out.shape[1]:
                break
            total = keep[index] + arrived[index].astype(F32)
            out[:, start : start + width] = total.astype(out.dtype)
            start += width


def tables_body(meta, lengths, dealing, inverse, ends, cosine, sine):
    rows, documents = dealing.shape
    quarters = (meta[1], 3 - meta[1])
    for row in range(rows):
        total = jnp.int32(0)
        for index in range(documents):
            total = total + lengths[row, dealing[row, index]]
            ends[row, index] = total
    sign = jnp.where((lanes_of((1, TILE)) % HD) < HD // 2, -1.0, 1.0)

    def one(block, carry):
        row = block // 2
        quarter = jnp.where(block % 2 == 0, quarters[0], quarters[1])
        point = quarter * 256 + lax.broadcasted_iota(jnp.int32, (256, 1), 0)
        begin = jnp.zeros((256, 1), jnp.int32)
        for index in range(documents):
            end = ends[row, index]
            begin = jnp.where(point >= end, end, begin)
        phase = (point - begin).astype(F32) * inverse[...]
        target = rows_at(block * 256, 256, 256)
        cosine[target, :] = jnp.cos(phase)
        sine[target, :] = jnp.sin(phase) * sign
        return carry

    lax.fori_loop(0, 2 * rows, one, 0)


def rotary_tables(meta, lengths, dealing):
    inverse = ROTARY_BASE ** (-(np.arange(HD // 2, dtype=np.float64) * 2.0 / HD))
    inverse = np.tile(inverse, 4).astype(np.float32)[None]
    rows, documents = dealing.shape
    table = jax.ShapeDtypeStruct((rows * 512, TILE), F32)
    return pl.pallas_call(
        tables_body,
        out_shape=[jax.ShapeDtypeStruct((rows, documents), jnp.int32), table, table],
        in_specs=[SMEM, SMEM, SMEM, VMEM],
        out_specs=[SMEM, VMEM, VMEM],
        compiler_params=pltpu.CompilerParams(vmem_limit_bytes=4 << 20),
        name="tables",
    )(meta, lengths, dealing, jnp.asarray(inverse))


def adam_step(gradient, master, moment, variance, decay, rate):
    moment_new = BETA_ONE * moment + (1.0 - BETA_ONE) * gradient
    variance_new = BETA_TWO * variance + (1.0 - BETA_TWO) * gradient * gradient
    first_fix = 1.0 - BETA_ONE**STEP
    second_fix = 1.0 - BETA_TWO**STEP
    stepped = (
        moment_new / first_fix / (jnp.sqrt(variance_new / second_fix) + ADAM_EPSILON)
        + decay * master
    )
    return (gradient, master - rate * stepped, moment_new, variance_new)


def swap_ctx(value):
    return lax.ppermute(value, "ctx", [(0, 1), (1, 0)])


def across(value, offset):
    return lax.ppermute(value, "tensor", [(i, i ^ offset) for i in range(PARTS)])


def shift_dp(value, shift):
    size = lax.axis_size("dp")
    return lax.ppermute(value, "dp", [(i, (i + shift) % size) for i in range(size)])


def spread_all(value):
    return [value] + [across(value, offset) for offset in range(1, PARTS)]


def spread_in_turn(value):
    half = value.shape[0] // 2
    first, second = across(value, 1), across(value, 2)
    return [value, first, second, across(second[:half], 1), across(first[half:], 2)]


def exchange(pieces):
    return [pieces[0]] + [across(pieces[offset], offset) for offset in range(1, PARTS)]


def after(value, *others):
    return lax.optimization_barrier((value, others))[0]


class Chain:
    def __init__(self, meta):
        self.meta = meta

    def call(self, name, body, outs, scalars, arrays, scratch=(), grown=None):
        results = call(name, body, outs, (self.meta, *scalars), arrays, scratch, grown)
        self.meta = after(self.meta, results[-1])
        return results


def gather_blocks(block):
    count = lax.axis_size("dp")
    return [block] + [shift_dp(block, shift) for shift in range(1, count)]


def stack_blocks(chain, pieces, split=1):
    shape = (len(pieces) // split, *pieces[0].shape)
    return chain.call("stack", stack_body, [(shape, BF16)] * split, (), pieces)


def context_sums(chain, *pairs, offsets=(0, 1, 2, 3), narrow=()):
    _, rows, first = pairs[0].shape
    width = sum(value.shape[2] for value in pairs[::2])
    outs = []
    for offset in offsets:
        size = first if offset in narrow else width
        outs.append(((rows, size), BF16 if offset else F32))
    body = functools.partial(context_sum_body, offsets)
    return chain.call("context_sum", body, outs, (), pairs)


def landed_blocks(sums):
    return [sums[0]] + [shift_dp(sums[shift], shift) for shift in range(1, len(sums))]


def per_device(
    tokens,
    cotangent,
    document_lengths,
    dealing,
    query_weight,
    query_master,
    query_moment,
    query_variance,
    keyvalue_weight,
    keyvalue_master,
    keyvalue_moment,
    keyvalue_variance,
    output_weight,
    output_master,
    output_moment,
    output_variance,
    gateup_weight,
    gateup_master,
    gateup_moment,
    gateup_variance,
    down_weight,
    down_master,
    down_moment,
    down_variance,
    norm_gain,
    gain_master,
    gain_moment,
    gain_variance,
):
    features = tokens.shape[-1]
    row_count = tokens.shape[0]
    block_rows = query_weight.shape[0]
    hidden_width = down_weight.shape[0]
    block_count = lax.axis_size("dp")
    part = lax.axis_index("tensor").astype(jnp.int32)
    context = lax.axis_index("ctx").astype(jnp.int32)
    own_dp = lax.axis_index("dp").astype(jnp.int32)
    meta = jnp.stack([part, context, own_dp, jnp.int32(0)])

    chain = Chain(meta)
    own_rows = row_count * 128
    count = row_count * 512
    own_tokens = tokens.reshape(own_rows, features)
    own_grad = cotangent.reshape(own_rows, features)
    by_hand = block_rows % 32 == 0 and block_count == 4
    half = own_rows // 2
    first_block, payload = chain.call(
        "prepare",
        prepare_body,
        [((block_rows, QKV), BF16), ((own_rows + 32, features), BF16)],
        (),
        (query_weight, keyvalue_weight, norm_gain, output_weight, own_tokens),
    )
    ends, cosine, sine = rotary_tables(chain.meta, document_lengths, dealing)

    token_pieces = spread_all(payload)
    if by_hand:
        first_pieces = [first_block] + [shift_dp(first_block, shift) for shift in (1, 2, 3)]
        first_own = stack_blocks(chain, after(first_pieces, cosine), 2)
        weight, gains = chain.call(
            "assemble_first",
            assemble_first_body,
            [((features, QKV), BF16), ((8, features), F32)],
            (),
            (*first_own, *[swap_ctx(value) for value in first_own]),
        )
    else:
        first_full = lax.all_gather(first_block, ("dp", "ctx"), axis=0, tiled=True)
        gains = jnp.pad(first_full[:, 3 * HD : 3 * HD + 2].T.astype(F32), ((0, 6), (0, 0)))
        lane = jnp.arange(QKV)
        weight = jnp.where((lane >= 3 * HD) & (lane < 4 * HD), 0, first_full).astype(BF16)
    second_block = chain.call(
        "join",
        join_body,
        [((block_rows, features + 3 * hidden_width), BF16)],
        (),
        (*token_pieces, gateup_weight, down_weight.T),
    )[0]
    done = (token_pieces[1:], weight)

    grads_x = across(after(own_grad, done), 1)
    grads_y = across(after(own_grad, done), 2)
    second_pieces = [second_block]
    if by_hand:
        second_pieces.append(shift_dp(after(second_block, done), 1))
    hidden, normed, query, keyval = chain.call(
        "project",
        project_body,
        [((count, features), BF16)] * 2 + [((count, 2 * TILE), BF16), ((count, 3 * TILE), BF16)],
        (),
        (
            *token_pieces,
            gains,
            after(weight, done),
            cosine,
            sine,
        ),
    )
    done = (grads_x, grads_y, second_pieces[1:])
    keyval_other = swap_ctx(after(keyval, done))
    done = (keyval_other,)

    grads_d = [
        across(after(grads_y, done)[:half], 1),
        across(after(grads_x, done)[half:], 2),
    ]
    if by_hand:
        second_third = shift_dp(after(second_block, done), 3)
    key_scratch = [((4, 256, 3 * TILE), BF16), ((4, 3 * TILE, 256), BF16), ((3, 256, 256), F32)]
    mixed, logs = chain.call(
        "attend",
        attend_body,
        [((row_count * 768, TILE), BF16), ((row_count * 2, 8, 256), F32)],
        (ends,),
        (after(query, done), keyval, keyval_other),
        key_scratch + [((3, 256, 256), F32)],
    )
    done = (grads_d, [second_third] if by_hand else [])

    head_pieces = spread_all(after(mixed, done))
    if by_hand:
        second_pieces += [shift_dp(after(second_block, done, mixed), 2), second_third]
        second_own = stack_blocks(chain, after(second_pieces, head_pieces))[0]
        second_full = chain.call(
            "assemble_second",
            assemble_second_body,
            [((features, features + 3 * hidden_width), BF16)],
            (),
            (second_own, swap_ctx(second_own)),
        )[0]
    else:
        second_full = lax.all_gather(second_block, ("dp", "ctx"), axis=0, tiled=True)
    piece_shape = ((own_rows, features), BF16)
    feed = chain.call(
        "feed",
        feed_body,
        [piece_shape] * 4
        + [
            ((count, features), BF16),
            ((count, hidden_width), BF16),
            ((count, 2 * hidden_width), BF16),
            ((count, features), BF16),
            ((own_rows, features), F32),
            ((own_rows, features), BF16),
        ],
        (ends,),
        (
            hidden,
            *head_pieces,
            own_grad,
            grads_x,
            grads_y,
            *grads_d,
            gains,
            second_full,
        ),
        [((256, features), BF16), ((256, features), BF16), ((256, features), F32)],
    )
    second, active, feed_grads, spread, middle_own, heads_own = feed[4:]

    def block_outs(width):
        if by_hand:
            shape = (block_count, block_rows, width)
            return [(shape, F32), (shape, BF16)]
        return [((features, width), BF16)]

    second_grads = exchange(feed[:4])
    feed_sums = chain.call(
        "feed_weights",
        feed_weights_body,
        block_outs(3 * hidden_width),
        (),
        (second, feed_grads, active, spread),
        [((features, count), BF16), ((features, count), BF16), ((features, 256), F32)],
    )
    if by_hand:
        feed_parts = context_sums(chain, feed_sums[0], swap_ctx(feed_sums[1]))
    fed = chain.call(
        "fed",
        fed_body,
        [piece_shape] * 4,
        (),
        (active, second_full),
        [((256, features), BF16)],
    )
    feed_landed = []
    if by_hand:
        feed_landed = [feed_parts[0]]
        feed_landed.append(shift_dp(after(feed_parts[2], fed[0]), 2))
        middle_own = after(middle_own, feed_landed[1:])
    sends = chain.call(
        "middle",
        middle_body,
        [((row_count * 192, TILE), BF16)] * 4
        + [((own_rows, features), F32), ((own_rows, features), BF16), ((8, features), F32)],
        (ends,),
        (*second_grads, middle_own, own_grad, gains, second_full),
    )
    grad_middle, grad_low, gain_two = sends[4:]
    grad_heads = exchange(sends[:4])
    output_sums = chain.call(
        "output_weights",
        output_weights_body,
        block_outs(features),
        (),
        (grad_low, heads_own),
        [((features, 256), F32)],
    )
    done = (grad_heads,)

    fed_near = [across(after(fed[offset], done), offset) for offset in (1, 2)]
    if by_hand:
        feed_landed.append(shift_dp(after(feed_parts[1], done), 1))
        arrived_output = swap_ctx(after(output_sums[1], done))
    else:
        arrived_output = grad_low
    grad_query, grad_own, grad_other = chain.call(
        "attend_back",
        attend_back_body,
        [((count, 2 * TILE), BF16), ((count, 3 * TILE), F32), ((count, 3 * TILE), BF16)],
        (ends,),
        (query, keyval, keyval_other, *grad_heads, logs, cosine, sine),
        key_scratch
        + [
            ((2, 256, 2 * TILE), BF16),
            ((3, 256, 256), F32),
            ((3, 256, 256), F32),
            ((4, 256, 3 * TILE), F32),
        ],
    )
    done = (fed_near, arrived_output, feed_landed[2:])
    arrived = swap_ctx(after(grad_other, done))

    fed_far = across(after(fed[3], arrived), 3)
    if by_hand:
        feed_landed.append(shift_dp(after(feed_parts[3], arrived), 3))
        pair = (output_sums[0], after(arrived_output, arrived))
        output_far = shift_dp(context_sums(chain, *pair, offsets=(2,))[0], 2)
    grads = chain.call(
        "first",
        first_body,
        [((count, QKV), BF16)],
        (),
        (grad_query, grad_own, arrived, cosine, sine),
    )[0]
    first_sums = chain.call(
        "first_weights",
        first_weights_body,
        block_outs(QKV),
        (),
        (normed, grads, weight, gains, gain_two),
        [((features, QKV), F32), ((features, count), BF16)],
    )
    spread_grads = chain.call(
        "spread_grad",
        spread_grad_body,
        [piece_shape] * PARTS,
        (),
        (grads, weight),
        [((QKV, features), BF16), ((256, features), BF16)],
    )
    done = (fed_far, feed_landed[3:], [output_far] if by_hand else [])
    first_grads = exchange(after(spread_grads, done))
    arrived_first = swap_ctx(after(first_sums[1], spread_grads, done)) if by_hand else grads
    if by_hand:
        last_parts = context_sums(
            chain, first_sums[0], arrived_first, output_sums[0], arrived_output, narrow=(2,)
        )
        feed_total = after(feed_landed[0], last_parts)
        for piece in feed_landed[1:]:
            feed_total = feed_total + piece.astype(F32)
        last_landed = [last_parts[0]] + [shift_dp(last_parts[k], k) for k in (2, 1)]
        last_landed.append(shift_dp(after(last_parts[3], first_grads[1]), 3))
        last_landed.append(output_far)
    else:
        scatter = functools.partial(
            lax.psum_scatter, axis_name=("dp", "ctx"), scatter_dimension=0, tiled=True
        )
        last_landed = [scatter(jnp.concatenate([first_sums[0], output_sums[0]], axis=1))]
        feed_total = scatter(feed_sums[0]).astype(F32)
    input_grad = chain.call(
        "input",
        input_body,
        [((own_rows, features), F32)],
        (),
        (*first_grads, own_tokens, grad_middle, gains),
    )[0].reshape(tokens.shape)
    packed_shape = (block_rows + 16, HEADS * HD)
    first_total, *packed = chain.call(
        "collect",
        collect_body,
        [((block_rows, QKV), F32)] + [(packed_shape, BF16)] * PARTS,
        (),
        last_landed,
    )
    landed = exchange(packed)
    block_output = after(middle_own, last_landed[0])
    fed_all = (fed[0], *fed_near, fed_far)
    for piece in fed_all:
        block_output = block_output + piece.astype(F32)
    block_output = block_output.astype(BF16).reshape(tokens.shape)
    output_results = chain.call(
        "finish",
        finish_body,
        [(output_weight.shape, F32)] * 4 + [(gain_master.shape, F32)] * 4,
        (),
        (
            *landed,
            output_master,
            output_moment,
            output_variance,
            gain_master,
            gain_moment,
            gain_variance,
        ),
    )

    query_grad = first_total[:, : HEADS * HD]
    key_tiles = [first_total[:, (2 + h) * TILE : (3 + h) * TILE] for h in range(HEADS)]
    keyvalue_grad = jnp.stack(
        [
            jnp.concatenate([tile[:, :HD] for tile in key_tiles], axis=1),
            jnp.concatenate([tile[:, HD:] for tile in key_tiles], axis=1),
        ]
    )
    gateup_grad = jnp.stack(
        [feed_total[:, :hidden_width], feed_total[:, hidden_width : 2 * hidden_width]]
    )
    down_grad = feed_total[:, 2 * hidden_width :].T
    return (
        block_output,
        input_grad,
        *adam_step(
            query_grad, query_master, query_moment, query_variance, WEIGHT_DECAY, LEARNING_RATE
        ),
        *adam_step(
            keyvalue_grad,
            keyvalue_master,
            keyvalue_moment,
            keyvalue_variance,
            WEIGHT_DECAY,
            LEARNING_RATE,
        ),
        *output_results[:4],
        *adam_step(
            gateup_grad, gateup_master, gateup_moment, gateup_variance, WEIGHT_DECAY, LEARNING_RATE
        ),
        *adam_step(
            down_grad, down_master, down_moment, down_variance, WEIGHT_DECAY, LEARNING_RATE
        ),
        *output_results[4:],
    )


def solution(mesh):
    hidden = P("dp", "ctx", None, "tensor", None)
    rows = P(("dp", "ctx"), "tensor")
    stacked = P(None, ("dp", "ctx"), "tensor")
    columns = P("tensor", ("dp", "ctx"))
    gain = P(None, ("dp", "ctx", "tensor"))
    return jax.shard_map(
        per_device,
        mesh=mesh,
        in_specs=(
            (hidden, hidden, P("dp", None), P("dp", None))
            + (rows,) * 4
            + (stacked,) * 4
            + (columns,) * 4
            + (stacked,) * 4
            + (columns,) * 4
            + (P(None, ("dp", "ctx")),)
            + (gain,) * 3
        ),
        out_specs=(
            (hidden, hidden)
            + (rows,) * 4
            + (stacked,) * 4
            + (columns,) * 4
            + (stacked,) * 4
            + (columns,) * 4
            + (gain,) * 4
        ),
        check_vma=False,
    )
```

```python
import functools

import jax
import jax.numpy as jnp
import numpy as np
from jax import lax
from jax.experimental import pallas as pl
from jax.experimental.pallas import tpu as pltpu
from jax.sharding import PartitionSpec as P

H = 12
HD = 64
STEP = 10
PARTS = 4
HEADS = H // PARTS
TILE = 2 * HD
QKV = 5 * TILE

EPSILON = 1e-05
BETA_ONE = 0.9
BETA_TWO = 0.95
ADAM_EPSILON = 1e-08
WEIGHT_DECAY = 0.1
LEARNING_RATE = 0.01
OUTPUT_RATE = 0.08
GAIN_RATE = 0.4
ROTARY_BASE = 10000.0
NEGATIVE = -1e30

F32 = jnp.float32
BF16 = jnp.bfloat16
VMEM_LIMIT = {}
FROM_HBM = ('prepare',)
SMEM = pl.BlockSpec(memory_space=pltpu.SMEM)
VMEM = pl.BlockSpec(memory_space=pltpu.VMEM)


def call(name, body, outs, scalars, arrays, scratch=(), grown=None):
    extra = () if grown is None else (grown,)
    out_shape = [jax.ShapeDtypeStruct(shape, dtype) for shape, dtype in outs]
    out_shape += [jax.ShapeDtypeStruct(value.shape, value.dtype) for value in extra]
    anywhere = [pl.BlockSpec(memory_space=pl.ANY) for _ in extra]
    scratch_shapes = [pltpu.VMEM(shape, dtype) for shape, dtype in scratch]
    if extra:
        scratch_shapes.append(pltpu.SemaphoreType.DMA(()))
    if name in FROM_HBM:
        arrays = [pltpu.with_memory_space_constraint(value, pltpu.HBM) for value in arrays]
    position = len(scalars) + len(arrays)
    return pl.pallas_call(
        body,
        out_shape=out_shape,
        in_specs=[SMEM] * len(scalars) + [VMEM] * len(arrays) + anywhere,
        out_specs=[VMEM] * len(outs) + anywhere,
        scratch_shapes=scratch_shapes,
        input_output_aliases={position: len(outs)} if extra else {},
        compiler_params=pltpu.CompilerParams(vmem_limit_bytes=VMEM_LIMIT.get(name, 8) << 20),
        name=name,
    )(*scalars, *arrays, *extra)


def dot(left, right):
    return lax.dot_general(left, right, (((1,), (0,)), ((), ())), preferred_element_type=F32)


def dot_nt(left, right):
    return lax.dot_general(left, right, (((1,), (1,)), ((), ())), preferred_element_type=F32)


def dot_tn(left, right):
    return lax.dot_general(left, right, (((0,), (0,)), ((), ())), preferred_element_type=F32)


def rows_at(start, size, unit):
    return pl.ds(pl.multiple_of(start, unit), size)


def lanes_of(shape):
    return lax.broadcasted_iota(jnp.int32, shape, len(shape) - 1)


def swapped(tile):
    first = (lanes_of(tile.shape) % HD) < HD // 2
    return jnp.where(first, pltpu.roll(tile, TILE - HD // 2, 1), pltpu.roll(tile, HD // 2, 1))


def root_mean(values):
    return lax.rsqrt(jnp.mean(values * values, axis=-1, keepdims=True) + EPSILON)


def wide_places(rows):
    places = []
    for index in range(0, -(-rows // 32)):
        size = min(32, rows - index * 32)
        source = slice(index * 32, index * 32 + size)
        tail = (3 + index // 2) * TILE + (index % 2) * HD
        places.append((source, size, index * TILE, tail))
    return places


def prepare_body(meta, query, keyvalue, gain, output, tokens, first, payload):
    rows, width = query.shape
    first[:, :width] = query[...]
    gains = jnp.concatenate([gain[...].astype(F32), jnp.zeros((HD - 2, rows), F32)], axis=0)
    first[:, width : width + HD] = gains.T.astype(BF16)
    for head in range(HEADS):
        start = (2 + head) * TILE
        lanes = slice(head * HD, (head + 1) * HD)
        first[:, start : start + TILE] = jnp.concatenate(
            [keyvalue[0, :, lanes], keyvalue[1, :, lanes]], axis=1
        )
    count = tokens.shape[0]
    payload[:count, :] = tokens[...]
    payload[count:, :] = jnp.zeros((32, tokens.shape[1]), BF16)
    turned = output[...].astype(F32).T.astype(BF16)
    for source, size, head, tail in wide_places(rows):
        payload[count : count + size, head : head + TILE] = turned[source, :TILE]
        payload[count : count + size, tail : tail + HD] = turned[source, TILE:]


def join_body(meta, p0, p1, p2, p3, gateup, down, out):
    rows, hidden = down.shape
    for source, size, head, tail in wide_places(rows):
        for index, piece in enumerate((p0, p1, p2, p3)):
            start = piece.shape[0] - 32
            lanes = slice(index * TILE, (index + 1) * TILE)
            out[source, lanes] = piece[start : start + size, head : head + TILE]
            rest = PARTS * TILE + index * HD
            out[source, rest : rest + HD] = piece[start : start + size, tail : tail + HD]
    width = PARTS * (TILE + HD)
    out[:, width : width + hidden] = gateup[0]
    out[:, width + hidden : width + 2 * hidden] = gateup[1]
    out[:, width + 2 * hidden :] = down[...]


def stack_body(meta, *refs):
    count = next(k for k in range(1, len(refs)) if refs[k].ndim == 3)
    pieces, outs = refs[:count], refs[count:]
    size = outs[0].shape[0]
    for shift, piece in enumerate(pieces):
        index = lax.rem(meta[2] + count - shift, count)
        for number, out in enumerate(outs):
            if len(outs) == 1:
                out[index] = piece[...]
            else:

                @pl.when(index // size == number)
                def _(out=out, piece=piece, index=index):
                    out[lax.rem(index, size)] = piece[...]


def assemble(meta, own, other, target, low, high, first=0):
    context = meta[1]
    count, rows, _ = own.shape
    for index in range(count):
        start = 2 * (first + index)
        target[rows_at((start + context) * rows, rows, 16), :] = own[index, :, low:high]
        target[rows_at((start + 1 - context) * rows, rows, 16), :] = other[index, :, low:high]


def assemble_second_body(meta, own, other, out):
    assemble(meta, own, other, out, 0, out.shape[1])


def assemble_first_body(meta, *refs):
    *parts, weight, gains = refs
    half = len(parts) // 2
    first = 0
    for own, other in zip(parts[:half], parts[half:]):
        assemble(meta, own, other, weight, 0, QKV, first)
        first += own.shape[0]
    tile = weight[:, TILE : 2 * TILE].astype(F32)
    gains[...] = tile.T[HD : HD + 8, :]
    weight[:, TILE : 2 * TILE] = jnp.where(lanes_of(tile.shape) < HD, tile, 0.0).astype(BF16)


def project_body(meta, x0, x1, x2, x3, gains, weight, cosine, sine, hidden, normed, query, keyval):
    part = meta[0]
    blocks = hidden.shape[0] // 256
    gain = gains[0:1, :]
    for offset, piece in enumerate((x0, x1, x2, x3)):
        place = jnp.bitwise_xor(part, offset)

        def spread(block, carry, piece=piece, place=place):
            source = piece[rows_at(block * 64, 64, 64), :]
            values = source.astype(F32)
            target = rows_at(block * 256 + place * 64, 64, 64)
            hidden[target, :] = source
            normed[target, :] = (values * root_mean(values) * gain).astype(BF16)
            return carry

        lax.fori_loop(0, blocks, spread, 0)

    def rotate(block, carry):
        rows = rows_at(block * 256, 256, 256)
        raw = dot(normed[rows, :], weight[...])
        cos, sin = cosine[rows, :], sine[rows, :]
        lower = lanes_of(cos.shape) < HD
        for index in range(5):
            tile = raw[:, index * TILE : (index + 1) * TILE]
            turned = tile * cos + swapped(tile) * sin
            lanes = slice((index - 2) * TILE, (index - 1) * TILE)
            if index < 2:
                query[rows, index * TILE : (index + 1) * TILE] = (turned * HD**-0.5).astype(BF16)
            else:
                keyval[rows, lanes] = jnp.where(lower, turned, tile).astype(BF16)
        return carry

    lax.fori_loop(0, blocks, rotate, 0)


def gather_keys(context, row, own, other, absolute):
    for side in range(2):
        rows = rows_at(row * 512 + side * 256, 256, 256)
        mine = context if side == 0 else 3 - context
        theirs = 1 - context if side == 0 else 2 + context
        absolute[mine] = own[rows, :]
        absolute[theirs] = other[rows, :]


def mask_bias(ends, row, query_quarter, key_quarter, documents):
    query_point = query_quarter * 256 + lax.broadcasted_iota(jnp.int32, (1, 256), 1)
    begin = jnp.zeros((1, 256), jnp.int32)
    for index in range(documents):
        end = ends[row, index]
        begin = jnp.where(query_point >= end, jnp.maximum(begin, end), begin)
    key_point = key_quarter * 256 + lax.broadcasted_iota(jnp.int32, (256, 256), 0)
    return jnp.where((key_point <= query_point) & (key_point >= begin), 0.0, NEGATIVE)


def query_pads(tiles):
    first, second = tiles[:, :TILE].astype(F32), tiles[:, TILE:].astype(F32)
    lower = lanes_of(first.shape) < HD
    return [
        jnp.where(lower, first, 0.0).astype(BF16),
        jnp.where(lower, pltpu.roll(first, HD, 1), 0.0).astype(BF16),
        jnp.where(lower, second, 0.0).astype(BF16),
    ]


def attend_body(meta, ends, query, own, other, mixed, logs, keys, keys_turned, bias, scores):
    context = meta[1]
    documents = ends.shape[1]

    def one(row, carry):
        gather_keys(context, row, own, other, keys)
        for quarter in range(4):
            for head in range(HEADS):
                lanes = slice(head * TILE, (head + 1) * TILE)
                keys_turned[quarter, lanes, :] = keys[quarter, :, lanes].astype(F32).T.astype(BF16)
        outs = []
        for side in range(2):
            quarter = context if side == 0 else 3 - context
            count = 2 + side
            base = 0 if side == 0 else 1 - context
            rows = rows_at(row * 512 + side * 256, 256, 256)
            for step in range(count):
                bias[step] = mask_bias(ends, meta[3] + row, quarter, base + step, documents)
            pads = query_pads(query[rows, :])
            turned = []
            for head in range(HEADS):
                lanes = slice(head * TILE, (head + 1) * TILE)
                highest = jnp.full((1, 256), NEGATIVE, F32)
                for step in range(count):
                    value = dot_nt(keys[base + step, :, lanes], pads[head]) + bias[step]
                    scores[step] = value
                    highest = jnp.maximum(highest, jnp.max(value, axis=0, keepdims=True))
                total = jnp.zeros((1, 256), F32)
                for step in range(count):
                    value = jnp.exp(scores[step] - highest)
                    scores[step] = value
                    total = total + jnp.sum(value, axis=0, keepdims=True)
                inverse = 1.0 / total
                result = jnp.zeros((TILE, 256), F32)
                for step in range(count):
                    weights = (scores[step] * inverse).astype(BF16)
                    result = result + dot(keys_turned[base + step, lanes, :], weights)
                turned.append(result[HD:, :])
                logs[2 * row + side, head : head + 1, :] = highest + jnp.log(total)
            pair = jnp.concatenate(turned[:2], axis=0)
            mixed[rows_at(row * 768 + side * 256, 256, 256), :] = pair.T.astype(BF16)
            outs.append(turned[2])
        packed = jnp.concatenate(outs, axis=0)
        mixed[rows_at(row * 768 + 512, 256, 256), :] = packed.T.astype(BF16)
        return carry

    lax.fori_loop(0, query.shape[0] // 512, one, 0)


def silu_parts(gating):
    gate = 1.0 / (1.0 + jnp.exp(-gating))
    return gate, gating * gate


def joined_heads(row, side, heads, target, lower):
    start = side * 256
    for index in range(PARTS):
        target[:, index * TILE : (index + 1) * TILE] = heads[index][start : start + 256, :]
    for index in range(2):
        tail = slice(512, 768)
        left = heads[2 * index][tail, :].astype(F32)
        right = heads[2 * index + 1][tail, :].astype(F32)
        if side == 0:
            tile = jnp.where(lower, left, pltpu.roll(right, HD, 1))
        else:
            tile = jnp.where(lower, pltpu.roll(left, HD, 1), right)
        target[:, (PARTS + index) * TILE : (PARTS + index + 1) * TILE] = tile.astype(BF16)


def feed_body(
    meta, ends, hidden, h0, h1, h2, h3, c0, c1, c2, c3, c4, gains, wide,
    o0, o1, o2, o3, second, active, grads, spread, middle_own, heads_own,
    joined, block_grad, block_middle,
):
    part, context = meta[0], meta[1]
    features = hidden.shape[1]
    width = active.shape[1]
    output = wide.at[:, :features]
    gateup = wide.at[:, features : features + 2 * width]
    down = wide.at[:, features + 2 * width :]
    gain = gains[1:2, :]
    lower = lanes_of((256, TILE)) < HD
    row_count = hidden.shape[0] // 512
    for row in range(row_count):
        far = row >= row_count // 2
        shift = row_count // 2 if far else 0
        heads = [piece.at[row * 768 : row * 768 + 768, :] for piece in (h0, h1, h2, h3)]
        for side in range(2):
            block = 2 * row + side
            rows = slice(block * 256, block * 256 + 256)
            joined_heads(row, side, heads, joined, lower)
            for offset, piece in enumerate((c0, c1, c2, c4 if far else c3)):
                place = jnp.bitwise_xor(part, offset)
                target = rows_at(block * 256 + place * 64, 64, 64)
                source = (block - 2 * shift if offset == 3 else block) * 64
                spread[target, :] = piece[source : source + 64, :]
            quarter = context if side == 0 else 3 - context
            point = quarter * 256 + lax.broadcasted_iota(jnp.int32, (256, 1), 0)
            keep = point < ends[meta[3] + row, ends.shape[1] - 1]
            out_grad = jnp.where(keep, spread[rows, :].astype(F32), 0.0).astype(BF16)
            spread[rows, :] = out_grad
            middle = hidden[rows, :].astype(F32) + dot_nt(joined[...], output[...])
            block_middle[...] = middle
            normed = (middle * root_mean(middle) * gain).astype(BF16)
            second[rows, :] = normed
            own = slice(block * 64, block * 64 + 64)
            mine = rows_at(part * 64, 64, 64)
            middle_own[own, :] = block_middle[mine, :]
            heads_own[own, :] = joined[mine, :]
            gate_up = dot(normed, gateup[...])
            gating, upward = gate_up[:, :width], gate_up[:, width:]
            grad_active = dot(out_grad, down[...])
            gate, passed = silu_parts(gating)
            active[rows, :] = (passed * upward).astype(BF16)
            grads[rows, :width] = (
                grad_active * upward * gate * (1.0 + gating * (1.0 - gate))
            ).astype(BF16)
            grads[rows, width:] = (grad_active * passed).astype(BF16)
            block_grad[...] = dot_nt(grads[rows, :], gateup[...]).astype(BF16)
            for offset, piece in enumerate((o0, o1, o2, o3)):
                place = jnp.bitwise_xor(part, offset)
                piece[own, :] = block_grad[rows_at(place * 64, 64, 64), :]


def fed_body(meta, active, wide, o0, o1, o2, o3, block_out):
    part = meta[0]
    down = wide.at[:, wide.shape[1] - active.shape[1] :]
    for block in range(active.shape[0] // 256):
        rows = slice(block * 256, block * 256 + 256)
        block_out[...] = dot_nt(active[rows, :], down[...]).astype(BF16)
        for offset, piece in enumerate((o0, o1, o2, o3)):
            place = jnp.bitwise_xor(part, offset)
            piece[block * 64 : block * 64 + 64, :] = block_out[rows_at(place * 64, 64, 64), :]


def give_rows(context, total, tile, outs, lanes):
    if len(outs) == 2:
        tile[...] = total
        split_rows(context, tile, *outs, lanes)
    else:
        outs[0][:, lanes] = total.astype(BF16)


def split_rows(context, source, keep, send, lanes):
    count, rows, _ = keep.shape
    for index in range(count):
        keep[index, :, lanes] = source[rows_at((2 * index + context) * rows, rows, 32), :]
        send[index, :, lanes] = source[
            rows_at((2 * index + 1 - context) * rows, rows, 32), :
        ].astype(BF16)


def feed_weights_body(meta, second, grads, active, spread, *refs):
    outs, (left, right, tile) = refs[:-3], refs[-3:]
    for block in range(second.shape[0] // 256):
        rows = slice(block * 256, block * 256 + 256)
        left[:, rows] = second[rows, :].T
        right[:, rows] = spread[rows, :].T
    width = active.shape[1]
    for start in range(0, 3 * width, 256):
        if start < 2 * width:
            total = dot(left[...], grads[:, start : start + 256])
        else:
            total = dot(right[...], active[:, start - 2 * width : start - 2 * width + 256])
        give_rows(meta[1], total, tile, outs, slice(start, start + 256))


def middle_body(
    meta, ends, g0, g1, g2, g3, middle_ref, out_grad_ref, gains, wide,
    s0, s1, s2, s3, grad_ref, low_ref, gain_ref,
):
    part, context = meta[0], meta[1]
    total = g0[...].astype(F32) + g1[...].astype(F32) + g2[...].astype(F32) + g3[...].astype(F32)
    middle = middle_ref[...]
    scale = root_mean(middle)
    gain = gains[1:2, :]
    keeps = []
    for block in range(middle.shape[0] // 64):
        row, side = block // 2, block % 2
        quarter = context if side == 0 else 3 - context
        point = quarter * 256 + part * 64 + lax.broadcasted_iota(jnp.int32, (64, 1), 0)
        keeps.append(point < ends[meta[3] + row, ends.shape[1] - 1])
    keep = jnp.concatenate([value.astype(F32) for value in keeps], axis=0)
    out_grad = out_grad_ref[...].astype(F32) * keep
    scaled = gain * total
    inner = jnp.mean(scaled * middle, axis=-1, keepdims=True)
    grad = out_grad + scale * scaled - middle * (scale * scale * scale * inner)
    grad_ref[...] = grad
    low = grad.astype(BF16)
    low_ref[...] = low
    gain_ref[...] = jnp.broadcast_to(
        jnp.sum(total * middle * scale, axis=0, keepdims=True), gain_ref.shape
    )
    heads = dot(low, wide[:, : low.shape[1]])
    lower = lanes_of((64, TILE)) < HD
    for offset, piece in enumerate((s0, s1, s2, s3)):
        tail = PARTS + offset // 2
        for row in range(middle.shape[0] // 128):
            rows = slice(row * 128, row * 128 + 128)
            piece[row * 192 : row * 192 + 128, :] = heads[
                rows, offset * TILE : (offset + 1) * TILE
            ].astype(BF16)
            former = heads[row * 128 : row * 128 + 64, tail * TILE : (tail + 1) * TILE]
            latter = heads[row * 128 + 64 : row * 128 + 128, tail * TILE : (tail + 1) * TILE]
            if offset % 2 == 0:
                packed = jnp.where(lower, former, pltpu.roll(latter, HD, 1))
            else:
                packed = jnp.where(lower, pltpu.roll(former, HD, 1), latter)
            piece[row * 192 + 128 : row * 192 + 192, :] = packed.astype(BF16)


def output_weights_body(meta, low, heads, *refs):
    outs, tile = refs[:-1], refs[-1]
    turned = low[...].T
    for start in range(0, heads.shape[1], 256):
        total = dot(turned, heads[:, start : start + 256])
        give_rows(meta[1], total, tile, outs, slice(start, start + 256))


def attend_back_body(
    meta, ends, query, own, other, g0, g1, g2, g3, logs, cosine, sine,
    grad_query, grad_own, grad_other, keys, keys_turned, bias, grad_heads, probs, grad_probs, sums,
):
    part, context = meta[0], meta[1]
    documents = ends.shape[1]

    def one(row, carry):
        gather_keys(context, row, own, other, keys)
        sums[...] = jnp.zeros_like(sums)
        for quarter in range(4):
            for head in range(HEADS):
                lanes = slice(head * TILE, (head + 1) * TILE)
                keys_turned[quarter, lanes, :] = keys[quarter, :, lanes].astype(F32).T.astype(BF16)
        for offset, piece in enumerate((g0, g1, g2, g3)):
            place = jnp.bitwise_xor(part, offset)
            for side in range(2):
                start = row * 192 + side * 64
                grad_heads[side, rows_at(place * 64, 64, 64), :TILE] = piece[rows_at(start, 64, 64), :]
            grad_heads[0, rows_at(place * 64, 64, 64), TILE:] = piece[
                rows_at(row * 192 + 128, 64, 64), :
            ]
        for side in range(2):
            quarter = context if side == 0 else 3 - context
            count = 2 + side
            base = 0 if side == 0 else 1 - context
            rows = rows_at(row * 512 + side * 256, 256, 256)
            for step in range(count):
                bias[step] = mask_bias(ends, meta[3] + row, quarter, base + step, documents)
            pads = query_pads(query[rows, :])
            first = grad_heads[side, :, :TILE].astype(F32)
            second = grad_heads[0, :, TILE:].astype(F32)
            upper = lanes_of(first.shape) >= HD
            tail = pltpu.roll(second, HD, 1) if side == 0 else second
            grads = [
                jnp.where(upper, pltpu.roll(first, HD, 1), 0.0).astype(BF16),
                jnp.where(upper, first, 0.0).astype(BF16),
                jnp.where(upper, tail, 0.0).astype(BF16),
            ]
            turned = []
            for head in range(HEADS):
                lanes = slice(head * TILE, (head + 1) * TILE)
                log = logs[2 * row + side, head : head + 1, :]
                inner = jnp.zeros((1, 256), F32)
                for step in range(count):
                    block = keys[base + step, :, lanes]
                    chance = jnp.exp(dot_nt(block, pads[head]) + bias[step] - log)
                    slope = dot_nt(block, grads[head])
                    probs[step] = chance
                    grad_probs[step] = slope
                    inner = inner + jnp.sum(chance * slope, axis=0, keepdims=True)
                sides = jnp.concatenate([pads[head], grads[head]], axis=0)
                result = jnp.zeros((TILE, 256), F32)
                for step in range(count):
                    chance = probs[step]
                    slope = (chance * (grad_probs[step] - inner)).astype(BF16)
                    both = jnp.concatenate([slope, chance.astype(BF16)], axis=1)
                    sums[base + step, :, lanes] += dot(both, sides)
                    result = result + dot(keys_turned[base + step, lanes, :], slope)
                turned.append(result[:HD, :])
            cos, sin = cosine[rows, :], sine[rows, :]
            turned.append(jnp.zeros((HD, 256), F32))
            for index in range(2):
                tile = jnp.concatenate(turned[2 * index : 2 * index + 2], axis=0).T * HD**-0.5
                grad_query[rows, index * TILE : (index + 1) * TILE] = (
                    tile * cos - swapped(tile) * sin
                ).astype(BF16)
        for side in range(2):
            rows = rows_at(row * 512 + side * 256, 256, 256)
            mine = context if side == 0 else 3 - context
            theirs = 1 - context if side == 0 else 2 + context
            grad_own[rows, :] = sums[mine]
            grad_other[rows, :] = sums[theirs].astype(BF16)
        return carry

    lax.fori_loop(0, query.shape[0] // 512, one, 0)


def first_body(meta, grad_query, grad_own, arrived, cosine, sine, grads):
    def one(block, carry):
        rows = rows_at(block * 256, 256, 256)
        cos, sin = cosine[rows, :], sine[rows, :]
        lower = lanes_of(cos.shape) < HD
        grads[rows, : 2 * TILE] = grad_query[rows, :]
        for index in range(HEADS):
            lanes = slice(index * TILE, (index + 1) * TILE)
            tile = grad_own[rows, lanes] + arrived[rows, lanes].astype(F32)
            turned = tile * cos - swapped(tile) * sin
            grads[rows, (2 + index) * TILE : (3 + index) * TILE] = jnp.where(
                lower, turned, tile
            ).astype(BF16)
        return carry

    lax.fori_loop(0, grad_query.shape[0] // 256, one, 0)


def spread_grad_body(meta, grads, weight, o0, o1, o2, o3, turned, block_grad):
    part = meta[0]
    turned[...] = weight[...].T
    for block in range(grads.shape[0] // 256):
        rows = slice(block * 256, block * 256 + 256)
        block_grad[...] = dot(grads[rows, :], turned[...]).astype(BF16)
        for offset, piece in enumerate((o0, o1, o2, o3)):
            place = jnp.bitwise_xor(part, offset)
            piece[block * 64 : block * 64 + 64, :] = block_grad[rows_at(place * 64, 64, 64), :]


def first_weights_body(meta, normed, grads, weight, gains, gain_two, *refs):
    outs, total, turned = refs[:-2], refs[-2], refs[-1]
    turned[...] = normed[...].T
    width = total.shape[1]
    for start, size in ((0, 256), (256, 384)):
        lanes = slice(start, start + size)
        total[:, lanes] = dot(turned[...], grads[:, lanes])
    product = total[...] * weight[...].astype(F32)
    column = jnp.sum(product, axis=1, keepdims=True)
    lane = lanes_of((normed.shape[1], TILE))
    row = lax.broadcasted_iota(jnp.int32, (TILE, normed.shape[1]), 0)
    two = jnp.where(row == HD + 1, gain_two[0:1, :], 0.0)
    one = jnp.where(row == HD, 1.0 / gains[0:1, :], 0.0)
    total[:, TILE : 2 * TILE] += two.T + one.T * column
    if len(outs) == 2:
        split_rows(meta[1], total, *outs, slice(0, width))
    else:
        outs[0][...] = total[...].astype(BF16)


def input_body(meta, g0, g1, g2, g3, tokens, grad_middle, gains, out):
    total = g0[...].astype(F32)
    for piece in (g1, g2, g3):
        total = total + piece[...].astype(F32)
    values = tokens[...].astype(F32)
    scale = root_mean(values)
    scaled = gains[0:1, :] * total
    inner = jnp.mean(scaled * values, axis=-1, keepdims=True)
    out[...] = grad_middle[...] + scale * scaled - values * (scale * scale * scale * inner)


def collect_body(meta, *refs):
    pieces, first, packed = refs[: -1 - PARTS], refs[-1 - PARTS], refs[-PARTS:]
    total, wide = None, None
    for piece in pieces:
        value = piece[...].astype(F32)
        if value.shape[1] != H * HD:
            total = value[:, :QKV] if total is None else total + value[:, :QKV]
            value = value[:, QKV:]
        if value.shape[1]:
            wide = value if wide is None else wide + value
    first[...] = total
    rows, width = total.shape[0], packed[0].shape[1]
    turned = total[:, TILE : 2 * TILE].T
    gains = jnp.concatenate([turned[HD : HD + 1, :], turned[HD + 1 : HD + 2, :]], axis=1)
    high = gains.astype(BF16)
    low = (gains - high.astype(F32)).astype(BF16)
    tail = jnp.concatenate([high, low, jnp.zeros((14, 2 * rows), BF16)], axis=0)
    for offset in range(PARTS):
        start = offset * TILE
        rest = PARTS * TILE + offset * HD
        packed[offset][:rows, :TILE] = wide[:, start : start + TILE].astype(BF16)
        packed[offset][:rows, TILE:] = wide[:, rest : rest + HD].astype(BF16)
        packed[offset][rows:, :] = jnp.pad(tail, ((0, 0), (0, width - 2 * rows)))


def finish_body(meta, p0, p1, p2, p3, *refs):
    output_states, gain_states = refs[:3], refs[3:6]
    output_outs, gain_outs = refs[6:10], refs[10:]
    total = p0[...].astype(F32) + p1[...].astype(F32) + p2[...].astype(F32) + p3[...].astype(F32)
    width, rows = output_outs[0].shape
    values = adam_step(
        total[:rows, :].T, *[ref[...] for ref in output_states], WEIGHT_DECAY, OUTPUT_RATE
    )
    for out, value in zip(output_outs, values):
        out[...] = value
    gains = total[rows : rows + 1, :] + total[rows + 1 : rows + 2, :]
    size = gain_outs[0].shape[1]
    picked = []
    for index in range(2):
        kept = jnp.zeros((1, size), F32)
        for place in range(PARTS):
            start = index * rows + place * size
            kept = jnp.where(meta[0] == place, gains[:, start : start + size], kept)
        picked.append(kept)
    values = adam_step(
        jnp.concatenate(picked, axis=0), *[ref[...] for ref in gain_states], 0.0, GAIN_RATE
    )
    for out, value in zip(gain_outs, values):
        out[...] = value


def context_sum_body(offsets, meta, *refs):
    pairs, outs = refs[: -len(offsets)], refs[-len(offsets) :]
    for offset, out in zip(offsets, outs):
        index = lax.rem(meta[2] + offset, pairs[0].shape[0])
        start = 0
        for keep, arrived in zip(pairs[::2], pairs[1::2]):
            width = keep.shape[2]
            if start + width > out.shape[1]:
                break
            total = keep[index] + arrived[index].astype(F32)
            out[:, start : start + width] = total.astype(out.dtype)
            start += width


def tables_body(meta, lengths, dealing, inverse, ends, cosine, sine):
    rows, documents = dealing.shape
    quarters = (meta[1], 3 - meta[1])
    for row in range(rows):
        total = jnp.int32(0)
        for index in range(documents):
            total = total + lengths[row, dealing[row, index]]
            ends[row, index] = total
    sign = jnp.where((lanes_of((1, TILE)) % HD) < HD // 2, -1.0, 1.0)

    def one(block, carry):
        row = block // 2
        quarter = jnp.where(block % 2 == 0, quarters[0], quarters[1])
        point = quarter * 256 + lax.broadcasted_iota(jnp.int32, (256, 1), 0)
        begin = jnp.zeros((256, 1), jnp.int32)
        for index in range(documents):
            end = ends[row, index]
            begin = jnp.where(point >= end, end, begin)
        phase = (point - begin).astype(F32) * inverse[...]
        target = rows_at(block * 256, 256, 256)
        cosine[target, :] = jnp.cos(phase)
        sine[target, :] = jnp.sin(phase) * sign
        return carry

    lax.fori_loop(0, 2 * rows, one, 0)


def rotary_tables(meta, lengths, dealing):
    inverse = ROTARY_BASE ** (-(np.arange(HD // 2, dtype=np.float64) * 2.0 / HD))
    inverse = np.tile(inverse, 4).astype(np.float32)[None]
    rows, documents = dealing.shape
    table = jax.ShapeDtypeStruct((rows * 512, TILE), F32)
    return pl.pallas_call(
        tables_body,
        out_shape=[jax.ShapeDtypeStruct((rows, documents), jnp.int32), table, table],
        in_specs=[SMEM, SMEM, SMEM, VMEM],
        out_specs=[SMEM, VMEM, VMEM],
        compiler_params=pltpu.CompilerParams(vmem_limit_bytes=4 << 20),
        name="tables",
    )(meta, lengths, dealing, jnp.asarray(inverse))


def adam_step(gradient, master, moment, variance, decay, rate):
    moment_new = BETA_ONE * moment + (1.0 - BETA_ONE) * gradient
    variance_new = BETA_TWO * variance + (1.0 - BETA_TWO) * gradient * gradient
    first_fix = 1.0 - BETA_ONE**STEP
    second_fix = 1.0 - BETA_TWO**STEP
    stepped = (
        moment_new / first_fix / (jnp.sqrt(variance_new / second_fix) + ADAM_EPSILON)
        + decay * master
    )
    return (gradient, master - rate * stepped, moment_new, variance_new)


def swap_ctx(value):
    return lax.ppermute(value, "ctx", [(0, 1), (1, 0)])


def across(value, offset):
    return lax.ppermute(value, "tensor", [(i, i ^ offset) for i in range(PARTS)])


def shift_dp(value, shift):
    size = lax.axis_size("dp")
    return lax.ppermute(value, "dp", [(i, (i + shift) % size) for i in range(size)])


def spread_all(value):
    return [value] + [across(value, offset) for offset in range(1, PARTS)]


def spread_in_turn(value):
    half = value.shape[0] // 2
    first, second = across(value, 1), across(value, 2)
    return [value, first, second, across(second[:half], 1), across(first[half:], 2)]


def exchange(pieces):
    return [pieces[0]] + [across(pieces[offset], offset) for offset in range(1, PARTS)]


def after(value, *others):
    return lax.optimization_barrier((value, others))[0]


class Chain:
    def __init__(self, meta):
        self.meta = meta

    def call(self, name, body, outs, scalars, arrays, scratch=(), grown=None):
        results = call(name, body, outs, (self.meta, *scalars), arrays, scratch, grown)
        self.meta = after(self.meta, results[-1])
        return results


def gather_blocks(block):
    count = lax.axis_size("dp")
    return [block] + [shift_dp(block, shift) for shift in range(1, count)]


def stack_blocks(chain, pieces, split=1):
    shape = (len(pieces) // split, *pieces[0].shape)
    return chain.call("stack", stack_body, [(shape, BF16)] * split, (), pieces)


def context_sums(chain, *pairs, offsets=(0, 1, 2, 3), narrow=()):
    _, rows, first = pairs[0].shape
    width = sum(value.shape[2] for value in pairs[::2])
    outs = []
    for offset in offsets:
        size = first if offset in narrow else width
        outs.append(((rows, size), BF16 if offset else F32))
    body = functools.partial(context_sum_body, offsets)
    return chain.call("context_sum", body, outs, (), pairs)


def landed_blocks(sums):
    return [sums[0]] + [shift_dp(sums[shift], shift) for shift in range(1, len(sums))]


def per_device(
    tokens,
    cotangent,
    document_lengths,
    dealing,
    query_weight,
    query_master,
    query_moment,
    query_variance,
    keyvalue_weight,
    keyvalue_master,
    keyvalue_moment,
    keyvalue_variance,
    output_weight,
    output_master,
    output_moment,
    output_variance,
    gateup_weight,
    gateup_master,
    gateup_moment,
    gateup_variance,
    down_weight,
    down_master,
    down_moment,
    down_variance,
    norm_gain,
    gain_master,
    gain_moment,
    gain_variance,
):
    features = tokens.shape[-1]
    row_count = tokens.shape[0]
    block_rows = query_weight.shape[0]
    hidden_width = down_weight.shape[0]
    block_count = lax.axis_size("dp")
    part = lax.axis_index("tensor").astype(jnp.int32)
    context = lax.axis_index("ctx").astype(jnp.int32)
    own_dp = lax.axis_index("dp").astype(jnp.int32)
    meta = jnp.stack([part, context, own_dp, jnp.int32(0)])

    chain = Chain(meta)
    own_rows = row_count * 128
    count = row_count * 512
    own_tokens = tokens.reshape(own_rows, features)
    own_grad = cotangent.reshape(own_rows, features)
    by_hand = block_rows % 32 == 0 and block_count == 4
    half = own_rows // 2
    first_block, payload = chain.call(
        "prepare",
        prepare_body,
        [((block_rows, QKV), BF16), ((own_rows + 32, features), BF16)],
        (),
        (query_weight, keyvalue_weight, norm_gain, output_weight, own_tokens),
    )
    ends, cosine, sine = rotary_tables(chain.meta, document_lengths, dealing)

    token_pieces = spread_all(payload)
    if by_hand:
        first_pieces = [first_block] + [shift_dp(first_block, shift) for shift in (1, 2, 3)]
        first_own = stack_blocks(chain, after(first_pieces, cosine), 2)
        weight, gains = chain.call(
            "assemble_first",
            assemble_first_body,
            [((features, QKV), BF16), ((8, features), F32)],
            (),
            (*first_own, *[swap_ctx(value) for value in first_own]),
        )
    else:
        first_full = lax.all_gather(first_block, ("dp", "ctx"), axis=0, tiled=True)
        gains = jnp.pad(first_full[:, 3 * HD : 3 * HD + 2].T.astype(F32), ((0, 6), (0, 0)))
        lane = jnp.arange(QKV)
        weight = jnp.where((lane >= 3 * HD) & (lane < 4 * HD), 0, first_full).astype(BF16)
    second_block = chain.call(
        "join",
        join_body,
        [((block_rows, features + 3 * hidden_width), BF16)],
        (),
        (*token_pieces, gateup_weight, down_weight.T),
    )[0]
    done = (token_pieces[1:], weight)

    grads_x = across(after(own_grad, done), 1)
    grads_y = across(after(own_grad, done), 2)
    second_pieces = [second_block]
    if by_hand:
        second_pieces.append(shift_dp(after(second_block, done), 1))
    hidden, normed, query, keyval = chain.call(
        "project",
        project_body,
        [((count, features), BF16)] * 2 + [((count, 2 * TILE), BF16), ((count, 3 * TILE), BF16)],
        (),
        (
            *token_pieces,
            gains,
            after(weight, done),
            cosine,
            sine,
        ),
    )
    done = (grads_x, grads_y, second_pieces[1:])
    keyval_other = swap_ctx(after(keyval, done))
    done = (keyval_other,)

    grads_d = [
        across(after(grads_y, done)[:half], 1),
        across(after(grads_x, done)[half:], 2),
    ]
    if by_hand:
        second_third = shift_dp(after(second_block, done), 3)
    key_scratch = [((4, 256, 3 * TILE), BF16), ((4, 3 * TILE, 256), BF16), ((3, 256, 256), F32)]
    mixed, logs = chain.call(
        "attend",
        attend_body,
        [((row_count * 768, TILE), BF16), ((row_count * 2, 8, 256), F32)],
        (ends,),
        (after(query, done), keyval, keyval_other),
        key_scratch + [((3, 256, 256), F32)],
    )
    done = (grads_d, [second_third] if by_hand else [])

    head_pieces = spread_all(after(mixed, done))
    if by_hand:
        second_pieces += [shift_dp(after(second_block, done, mixed), 2), second_third]
        second_own = stack_blocks(chain, after(second_pieces, head_pieces))[0]
        second_full = chain.call(
            "assemble_second",
            assemble_second_body,
            [((features, features + 3 * hidden_width), BF16)],
            (),
            (second_own, swap_ctx(second_own)),
        )[0]
    else:
        second_full = lax.all_gather(second_block, ("dp", "ctx"), axis=0, tiled=True)
    piece_shape = ((own_rows, features), BF16)
    feed = chain.call(
        "feed",
        feed_body,
        [piece_shape] * 4
        + [
            ((count, features), BF16),
            ((count, hidden_width), BF16),
            ((count, 2 * hidden_width), BF16),
            ((count, features), BF16),
            ((own_rows, features), F32),
            ((own_rows, features), BF16),
        ],
        (ends,),
        (
            hidden,
            *head_pieces,
            own_grad,
            grads_x,
            grads_y,
            *grads_d,
            gains,
            second_full,
        ),
        [((256, features), BF16), ((256, features), BF16), ((256, features), F32)],
    )
    second, active, feed_grads, spread, middle_own, heads_own = feed[4:]

    def block_outs(width):
        if by_hand:
            shape = (block_count, block_rows, width)
            return [(shape, F32), (shape, BF16)]
        return [((features, width), BF16)]

    second_grads = exchange(feed[:4])
    feed_sums = chain.call(
        "feed_weights",
        feed_weights_body,
        block_outs(3 * hidden_width),
        (),
        (second, feed_grads, active, spread),
        [((features, count), BF16), ((features, count), BF16), ((features, 256), F32)],
    )
    if by_hand:
        feed_parts = context_sums(chain, feed_sums[0], swap_ctx(feed_sums[1]))
    feed_landed = []
    if by_hand:
        feed_landed = [feed_parts[0]]
        feed_landed.append(shift_dp(feed_parts[2], 2))
        middle_own = after(middle_own, feed_landed[1:])
    sends = chain.call(
        "middle",
        middle_body,
        [((row_count * 192, TILE), BF16)] * 4
        + [((own_rows, features), F32), ((own_rows, features), BF16), ((8, features), F32)],
        (ends,),
        (*second_grads, middle_own, own_grad, gains, second_full),
    )
    grad_middle, grad_low, gain_two = sends[4:]
    grad_heads = exchange(sends[:4])
    fed = chain.call(
        "fed",
        fed_body,
        [piece_shape] * 4,
        (),
        (active, second_full),
        [((256, features), BF16)],
    )
    output_sums = chain.call(
        "output_weights",
        output_weights_body,
        block_outs(features),
        (),
        (grad_low, heads_own),
        [((features, 256), F32)],
    )
    done = (grad_heads,)
    if by_hand:
        feed_landed.append(shift_dp(after(feed_parts[3], grad_low), 3))
        done = (grad_heads, feed_landed[2:])

    fed_near = [across(after(fed[offset], done), offset) for offset in (1, 2)]
    if by_hand:
        feed_landed.append(shift_dp(after(feed_parts[1], done), 1))
        arrived_output = swap_ctx(after(output_sums[1], done))
    else:
        arrived_output = grad_low
    grad_query, grad_own, grad_other = chain.call(
        "attend_back",
        attend_back_body,
        [((count, 2 * TILE), BF16), ((count, 3 * TILE), F32), ((count, 3 * TILE), BF16)],
        (ends,),
        (query, keyval, keyval_other, *grad_heads, logs, cosine, sine),
        key_scratch
        + [
            ((2, 256, 2 * TILE), BF16),
            ((3, 256, 256), F32),
            ((3, 256, 256), F32),
            ((4, 256, 3 * TILE), F32),
        ],
    )
    done = (fed_near, arrived_output, feed_landed[3:])
    arrived = swap_ctx(after(grad_other, done))

    fed_far = across(after(fed[3], arrived), 3)
    if by_hand:
        pair = (output_sums[0], after(arrived_output, arrived))
        output_far = shift_dp(context_sums(chain, *pair, offsets=(2,))[0], 2)
    grads = chain.call(
        "first",
        first_body,
        [((count, QKV), BF16)],
        (),
        (grad_query, grad_own, arrived, cosine, sine),
    )[0]
    first_sums = chain.call(
        "first_weights",
        first_weights_body,
        block_outs(QKV),
        (),
        (normed, grads, weight, gains, gain_two),
        [((features, QKV), F32), ((features, count), BF16)],
    )
    spread_grads = chain.call(
        "spread_grad",
        spread_grad_body,
        [piece_shape] * PARTS,
        (),
        (grads, weight),
        [((QKV, features), BF16), ((256, features), BF16)],
    )
    done = (fed_far, [output_far] if by_hand else [])
    first_grads = exchange(after(spread_grads, done))
    arrived_first = swap_ctx(after(first_sums[1], spread_grads, done)) if by_hand else grads
    if by_hand:
        last_parts = context_sums(
            chain, first_sums[0], arrived_first, output_sums[0], arrived_output, narrow=(2,)
        )
        feed_total = after(feed_landed[0], last_parts)
        for piece in feed_landed[1:]:
            feed_total = feed_total + piece.astype(F32)
        last_landed = [last_parts[0]] + [shift_dp(last_parts[k], k) for k in (2, 1)]
        last_landed.append(shift_dp(after(last_parts[3], first_grads[1]), 3))
        last_landed.append(output_far)
    else:
        scatter = functools.partial(
            lax.psum_scatter, axis_name=("dp", "ctx"), scatter_dimension=0, tiled=True
        )
        last_landed = [scatter(jnp.concatenate([first_sums[0], output_sums[0]], axis=1))]
        feed_total = scatter(feed_sums[0]).astype(F32)
    input_grad = chain.call(
        "input",
        input_body,
        [((own_rows, features), F32)],
        (),
        (*first_grads, own_tokens, grad_middle, gains),
    )[0].reshape(tokens.shape)
    packed_shape = (block_rows + 16, HEADS * HD)
    first_total, *packed = chain.call(
        "collect",
        collect_body,
        [((block_rows, QKV), F32)] + [(packed_shape, BF16)] * PARTS,
        (),
        last_landed,
    )
    landed = exchange(packed)
    block_output = after(middle_own, last_landed[0])
    fed_all = (fed[0], *fed_near, fed_far)
    for piece in fed_all:
        block_output = block_output + piece.astype(F32)
    block_output = block_output.astype(BF16).reshape(tokens.shape)
    output_results = chain.call(
        "finish",
        finish_body,
        [(output_weight.shape, F32)] * 4 + [(gain_master.shape, F32)] * 4,
        (),
        (
            *landed,
            output_master,
            output_moment,
            output_variance,
            gain_master,
            gain_moment,
            gain_variance,
        ),
    )

    query_grad = first_total[:, : HEADS * HD]
    key_tiles = [first_total[:, (2 + h) * TILE : (3 + h) * TILE] for h in range(HEADS)]
    keyvalue_grad = jnp.stack(
        [
            jnp.concatenate([tile[:, :HD] for tile in key_tiles], axis=1),
            jnp.concatenate([tile[:, HD:] for tile in key_tiles], axis=1),
        ]
    )
    gateup_grad = jnp.stack(
        [feed_total[:, :hidden_width], feed_total[:, hidden_width : 2 * hidden_width]]
    )
    down_grad = feed_total[:, 2 * hidden_width :].T
    return (
        block_output,
        input_grad,
        *adam_step(
            query_grad, query_master, query_moment, query_variance, WEIGHT_DECAY, LEARNING_RATE
        ),
        *adam_step(
            keyvalue_grad,
            keyvalue_master,
            keyvalue_moment,
            keyvalue_variance,
            WEIGHT_DECAY,
            LEARNING_RATE,
        ),
        *output_results[:4],
        *adam_step(
            gateup_grad, gateup_master, gateup_moment, gateup_variance, WEIGHT_DECAY, LEARNING_RATE
        ),
        *adam_step(
            down_grad, down_master, down_moment, down_variance, WEIGHT_DECAY, LEARNING_RATE
        ),
        *output_results[4:],
    )


def solution(mesh):
    hidden = P("dp", "ctx", None, "tensor", None)
    rows = P(("dp", "ctx"), "tensor")
    stacked = P(None, ("dp", "ctx"), "tensor")
    columns = P("tensor", ("dp", "ctx"))
    gain = P(None, ("dp", "ctx", "tensor"))
    return jax.shard_map(
        per_device,
        mesh=mesh,
        in_specs=(
            (hidden, hidden, P("dp", None), P("dp", None))
            + (rows,) * 4
            + (stacked,) * 4
            + (columns,) * 4
            + (stacked,) * 4
            + (columns,) * 4
            + (P(None, ("dp", "ctx")),)
            + (gain,) * 3
        ),
        out_specs=(
            (hidden, hidden)
            + (rows,) * 4
            + (stacked,) * 4
            + (columns,) * 4
            + (stacked,) * 4
            + (columns,) * 4
            + (gain,) * 4
        ),
        check_vma=False,
    )
```
